128 devices in a mesh: dp: 16 (over y, x_hi, core), rows: 8 (over z, x_lo).
Axes of the slice: x: 4 (x_hi: 2, x_lo: 2; x = x_hi * 2 + x_lo), y: 4, z: 4, core: 2. Of those that a mesh axis runs over, the one named last changes fastest.
Arguments:
- images: bfloat16 [16, 24, 48, 1280], P('dp', 'rows'), may hold values from -6 to 6
- cotangent: bfloat16 [16, 24, 48, 1280], P('dp', 'rows'), may hold values from -6 to 6
- first_weight: bfloat16 [16, 8, 9, 12800], P('dp', 'rows'), may hold values from -0.0546875 to 0.0546875
- second_weight: bfloat16 [16, 8, 9, 12800], P('dp', 'rows'), may hold values from -0.0546875 to 0.0546875
- first_basis: float32 [64, 1280], replicated, may hold values from -0.15625 to 0.15625
- second_basis: float32 [64, 1280], replicated, may hold values from -0.15625 to 0.15625
Outputs:
- block_output: bfloat16 [16, 24, 48, 1280], P('dp', 'rows')
- first_grad: float32 [16, 8, 9, 12800], P('dp', 'rows')
- second_grad: float32 [16, 8, 9, 12800], P('dp', 'rows')
The draws below stay inside these ranges and needn't reach their ends.
All inputs are finite; a program needn't handle non-finite values.
Results may differ from the reference program's by a relative error of at most 0.014.
Values may be sent and summed in bfloat16 or wider, within the bound.
A program may use at most 192 MiB of HBM per device.

```python
import math
import jax
import jax.numpy as jnp
from jax import lax

CHANNELS = 1280
GROUPS = 32
RANK = 64
LAT_W = 48
IMAGES = 16
LAT_H = 24
N_DP = 16
N_ROWS = 8


def strengthened(drawn, stream_key, source, target, blocks, factor):
    def block_of(axis_at):
        return (jnp.arange(drawn.shape[axis_at]) // (drawn.shape[axis_at] // blocks)).reshape((-1,) + (1,) * (drawn.ndim - 1 - axis_at))

    near = jax.random.permutation(stream_key, blocks)[block_of(target)]
    second = (block_of(target) + blocks // 2) % blocks
    return jnp.where((block_of(source) == near) | (block_of(source) == second), factor * drawn, drawn)


def steps_of(own_key, shape, pieces, smallest, top_value):
    level, own = 1.0, jax.random.fold_in(own_key, 6)
    for axis_at, parts in pieces:
        heights = jnp.exp(jax.random.uniform(jax.random.fold_in(own, axis_at), (parts,), jnp.float32, smallest / len(pieces), top_value / len(pieces)))
        level = level * jnp.repeat(heights, shape[axis_at] // parts).reshape([-1 if axis == axis_at else 1 for axis in range(len(shape))])
    return level


def normal_values(stream_key, dims, scale, bound, shards=(), kind=jnp.bfloat16):
    factor_of = steps_of(stream_key, dims, shards, -0.22, 0.18) if shards else 1.0
    values = jax.random.normal(stream_key, dims, jnp.float32) * scale * factor_of
    return jnp.minimum(jnp.maximum(values, -bound), bound).astype(kind)


def heavy_noise(own_key, extent, scale, most, pieces, heavy, held_as=jnp.bfloat16):
    entries = scale * jax.random.normal(own_key, extent, jnp.float32)
    if pieces:
        entries = entries * steps_of(own_key, extent, pieces, -0.22, 0.18)
    return jnp.clip(strengthened(entries, jax.random.fold_in(own_key, 3), *heavy), -most, most).astype(held_as)


def setup_inputs(seed: int = 0) -> dict:
    key_of = jax.random.split(jax.random.key(seed), 7)
    return {
        "images": normal_values(key_of[0], (IMAGES, LAT_H, LAT_W, CHANNELS), 1.0, 6.0, ((0, 16), (1, 8))),
        "cotangent": heavy_noise(key_of[1], (IMAGES, LAT_H, LAT_W, CHANNELS), 1.0, 6.0, ((0, 16), (1, 8)), (0, 3, 16, 2.0)),
        "first_weight": normal_values(key_of[2], (N_DP, N_ROWS, 9, (CHANNELS // N_DP) * (CHANNELS // N_ROWS)), (9 * CHANNELS) ** -0.5, 0.0546875, ((0, 16), (1, 8))),
        "second_weight": normal_values(key_of[3], (N_DP, N_ROWS, 9, (CHANNELS // N_DP) * (CHANNELS // N_ROWS)), (9 * CHANNELS) ** -0.5, 0.0546875, ((0, 16), (1, 8))),
        "first_basis": normal_values(key_of[4], (RANK, CHANNELS), CHANNELS ** -0.5, 0.15625, (), jnp.float32),
        "second_basis": normal_values(key_of[5], (RANK, CHANNELS), CHANNELS ** -0.5, 0.15625, (), jnp.float32),
    }


def normalize(values):
    full_shape = values.shape
    size_group = CHANNELS // GROUPS
    grouped = values.reshape(full_shape[:-1] + (full_shape[-1] // size_group, size_group))
    center = lax.optimization_barrier(jnp.mean(grouped, axis=(1, 2, 4), keepdims=True))
    spread = lax.optimization_barrier(jnp.mean(jnp.square(grouped - center), axis=(1, 2, 4), keepdims=True))
    return ((grouped - center) / jnp.sqrt(spread + 1e-05)).reshape(full_shape)

def activate(values):
    return jax.nn.silu(normalize(values))

def convolve(inputs, kernel):
    padded = jnp.pad(inputs.astype(jnp.float32), ((0, 0), (1, 1), (1, 1), (0, 0)))
    kernel_wide = kernel.astype(jnp.float32)
    height = inputs.shape[1]
    width = inputs.shape[2]
    summed = jnp.zeros(inputs.shape[:3] + (kernel.shape[3],), jnp.float32)
    for row_tap in range(3):
        for col_tap in range(3):
            window = padded[:, row_tap:row_tap + height, col_tap:col_tap + width]
            summed = summed + jnp.einsum('nhwc,cd->nhwd', window, kernel_wide[row_tap, col_tap])
    return summed

def weight_grad(inputs, grads):
    padded = jnp.pad(inputs.astype(jnp.float32), ((0, 0), (1, 1), (1, 1), (0, 0)))
    grads_wide = grads.astype(jnp.float32)
    height = inputs.shape[1]
    width = inputs.shape[2]
    taps = []
    for row_tap in range(3):
        row_list = []
        for col_tap in range(3):
            window = padded[:, row_tap:row_tap + height, col_tap:col_tap + width]
            row_list.append(jnp.einsum('nhwc,nhwd->cd', window, grads_wide))
        taps.append(jnp.stack(row_list))
    return jnp.stack(taps)

def project(raw_grad, basis):
    coefficient = jnp.einsum('abcd,rc->abrd', raw_grad, basis, precision=lax.Precision.HIGHEST)
    return raw_grad - jnp.einsum('rc,abrd->abcd', basis, coefficient, precision=lax.Precision.HIGHEST)

def first_kernel(flat):
    dp_width = CHANNELS // N_DP
    rows_width = CHANNELS // N_ROWS
    blocks = flat.reshape(N_DP, N_ROWS, 3, 3, dp_width, rows_width)
    return jnp.transpose(blocks, (2, 3, 0, 4, 1, 5)).reshape(3, 3, CHANNELS, CHANNELS)

def second_kernel(flat):
    dp_width = CHANNELS // N_DP
    rows_width = CHANNELS // N_ROWS
    blocks = flat.reshape(N_DP, N_ROWS, 3, 3, dp_width, rows_width)
    return jnp.transpose(blocks, (2, 3, 1, 5, 0, 4)).reshape(3, 3, CHANNELS, CHANNELS)

def first_flat(grad):
    dp_width = CHANNELS // N_DP
    rows_width = CHANNELS // N_ROWS
    blocks = grad.reshape(3, 3, N_DP, dp_width, N_ROWS, rows_width)
    return jnp.transpose(blocks, (2, 4, 0, 1, 3, 5)).reshape(N_DP, N_ROWS, 9, dp_width * rows_width)

def second_flat(grad):
    dp_width = CHANNELS // N_DP
    rows_width = CHANNELS // N_ROWS
    blocks = grad.reshape(3, 3, N_ROWS, rows_width, N_DP, dp_width)
    return jnp.transpose(blocks, (4, 2, 0, 1, 5, 3)).reshape(N_DP, N_ROWS, 9, dp_width * rows_width)

def reference(images, cotangent, first_weight, second_weight, first_basis, second_basis):
    grad_scale = 1.0 / math.sqrt(IMAGES * LAT_H * LAT_W)
    kernel_one = first_kernel(first_weight)
    kernel_two = second_kernel(second_weight)
    activated = activate(images.astype(jnp.float32)).astype(jnp.bfloat16)
    first_out = convolve(activated, kernel_one)
    hidden = activate(first_out).astype(jnp.bfloat16)
    second_out = convolve(hidden, kernel_two)
    block_output = (images.astype(jnp.float32) + second_out).astype(jnp.bfloat16)
    flipped = jnp.transpose(kernel_two[::-1, ::-1], (0, 1, 3, 2))
    hidden_grad = convolve(cotangent, flipped)
    unused, pullback = jax.vjp(activate, first_out)
    pre_grad = pullback(hidden_grad)[0].astype(jnp.bfloat16)
    raw_first = weight_grad(activated, pre_grad)
    raw_second = weight_grad(hidden, cotangent)
    first_grad = first_flat(project(raw_first, first_basis) * grad_scale)
    second_grad = second_flat(project(raw_second, second_basis) * grad_scale)
    return (block_output, first_grad, second_grad)
```

```python
import math

import jax
import jax.numpy as jnp
from jax import lax
from jax.experimental import pallas as pl
from jax.experimental.pallas import tpu as pltpu
from jax.sharding import PartitionSpec as P

C = 1280
GSIZE = 40
W = 48
H = 24
PIX = W * H
BAND = 144
DPW = 80
RW = 160
Q = 512
K3 = 3 * Q
RANK = 64
EPS = 1e-05
F32 = jnp.float32
BF16 = jnp.bfloat16
MESH = pl.DeviceIdType.MESH
HIGH = lax.Precision.HIGHEST
N_SEM = 104


def dot(a, b):
    return jnp.dot(a, b, preferred_element_type=F32)


def dot_nt(a, b):
    return lax.dot_general(a, b, (((1,), (1,)), ((), ())), preferred_element_type=F32)


def group_matrix(rows, channel_of):
    channel = channel_of(lax.broadcasted_iota(jnp.int32, (rows, 128), 0))
    group = lax.broadcasted_iota(jnp.int32, (rows, 128), 1) * GSIZE
    return jnp.where((channel >= group) & (channel < group + GSIZE), 1.0, 0.0).astype(F32)


def group_mean(sums, groups):
    per_group = jnp.sum(jnp.dot(sums, groups, precision=HIGH, preferred_element_type=F32), axis=0, keepdims=True)
    spread = lax.dot_general(
        jnp.broadcast_to(per_group, (8, 128)), groups, (((1,), (1,)), ((), ())),
        precision=HIGH, preferred_element_type=F32,
    )
    return spread[0:1] * (1.0 / (PIX * GSIZE))


def fold8(values):
    total = values[0:8]
    for at in range(8, values.shape[0], 8):
        total = total + values[at : at + 8]
    return total


def split(values):
    high = values.astype(BF16)
    low = (values - high.astype(F32)).astype(BF16)
    return high, low


def kernel(
    img, cot, w1r, w2r, b1, b2, out, g1, g2,
    imgf, cotp, w1, w2, actp, x, s, du, hidc, hp, pp, act_t, cot_t,
    o, qa, qb, qd, qv, hb, hx, hpair, gr, gc, gt, ga, gb, gd, gu, bs1, bs2,
    ssem, rsem,
):
    dp = lax.axis_index("dp")
    rows = lax.axis_index("rows")
    core = lax.rem(dp, 2)
    xh = lax.rem(dp // 2, 2)
    y = dp // 4
    xl = lax.rem(rows, 2)
    z = rows // 2
    zp, zm, z2 = lax.rem(z + 1, 4), lax.rem(z + 3, 4), lax.rem(z + 2, 4)
    yp, ym, y2 = lax.rem(y + 1, 4), lax.rem(y + 3, 4), lax.rem(y + 2, 4)
    ZP, ZM = (dp, zp * 2 + xl), (dp, zm * 2 + xl)
    XN = (dp, z * 2 + 1 - xl)
    YP, YM = (yp * 4 + xh * 2 + core, rows), (ym * 4 + xh * 2 + core, rows)
    XH = (y * 4 + (1 - xh) * 2 + core, rows)
    CN = (y * 4 + xh * 2 + 1 - core, rows)
    pending = []

    def send(src, dst, device):
        at = len(pending)
        copy = pltpu.make_async_remote_copy(
            src_ref=src, dst_ref=dst, send_sem=ssem.at[at], recv_sem=rsem.at[at],
            device_id=device, device_id_type=MESH,
        )
        copy.start()
        pending.append(copy)
        return copy

    def gather_rows(src, full, base):
        def at(zz, xx, low=0, size=BAND):
            return full.at[pl.ds(pl.multiple_of(base + (zz * 2 + xx) * BAND + low, 16), size)]

        def pass_on(piece, device):
            return send(piece, piece, device)

        own = at(z, xl)
        cx, cp, cm = send(src, own, XN), send(src, own, ZP), send(src, own, ZM)
        yield
        cx.wait_recv()
        ep, em = pass_on(at(z, 1 - xl), ZP), pass_on(at(z, 1 - xl), ZM)
        yield
        cp.wait_recv()
        fp = pass_on(at(zm, xl, 0, 80), ZP)
        cm.wait_recv()
        fm = pass_on(at(zp, xl, 80, 64), ZM)
        yield
        ep.wait_recv()
        hp_ = pass_on(at(zm, 1 - xl, 0, 80), ZP)
        em.wait_recv()
        hm_ = pass_on(at(zp, 1 - xl, 80, 64), ZM)
        yield
        for copy in (fp, fm, hp_, hm_):
            copy.wait_recv()
        yield

    def gather_weight(full):
        def at(yy, hh, low=0, size=DPW):
            return full.at[pl.ds(pl.multiple_of(((yy * 2 + hh) * 2 + core) * DPW + low, 16), size)]

        def pass_on(piece, device):
            return send(piece, piece, device)

        own = at(y, xh)
        ax, ap, am, ac = (pass_on(own, device) for device in (XH, YP, YM, CN))
        yield
        ax.wait_recv()
        bp, bm, bc = (pass_on(at(y, 1 - xh), device) for device in (YP, YM, CN))
        yield
        ap.wait_recv()
        fp, fc = pass_on(at(ym, xh, 0, 48), YP), pass_on(at(ym, xh), CN)
        am.wait_recv()
        fm, fd = pass_on(at(yp, xh, 48, 32), YM), pass_on(at(yp, xh), CN)
        yield
        bp.wait_recv()
        hp_, hc = pass_on(at(ym, 1 - xh, 0, 48), YP), pass_on(at(ym, 1 - xh), CN)
        bm.wait_recv()
        hm_, hd = pass_on(at(yp, 1 - xh, 48, 32), YM), pass_on(at(yp, 1 - xh), CN)
        yield
        last = []
        fp.wait_recv()
        last.append(pass_on(at(y2, xh, 0, 48), CN))
        fm.wait_recv()
        last.append(pass_on(at(y2, xh, 48, 32), CN))
        hp_.wait_recv()
        last.append(pass_on(at(y2, 1 - xh, 0, 48), CN))
        hm_.wait_recv()
        last.append(pass_on(at(y2, 1 - xh, 48, 32), CN))
        yield
        for copy in [ac, bc, fc, fd, hc, hd] + last:
            copy.wait_recv()
        yield

    scale = 1.0 / math.sqrt(16 * PIX)

    def scatter_grad(n, grad_out, p):
        c = send(gr.at[n, :, 1 - core], gc.at[n], CN)
        yield
        c.wait_recv()
        for block in range(8):
            gt[n, block] = (gr[n, block, core].astype(F32) + gc[n, block].astype(F32)).astype(BF16)
        ap = send(gt.at[n, y2 * 2], ga.at[n, 0], YP)
        am = send(gt.at[n, y2 * 2 + 1], ga.at[n, 1], YM)
        yield
        ap.wait_recv()
        gt[n, yp * 2] = (gt[n, yp * 2].astype(F32) + ga[n, 0].astype(F32)).astype(BF16)
        bp = send(gt.at[n, pl.ds(yp * 2, 2)], gb.at[n, 0], YP)
        am.wait_recv()
        gt[n, ym * 2 + 1] = (gt[n, ym * 2 + 1].astype(F32) + ga[n, 1].astype(F32)).astype(BF16)
        bm = send(gt.at[n, pl.ds(ym * 2, 2)], gb.at[n, 1], YM)
        yield
        bp.wait_recv()
        bm.wait_recv()

        def mine(h):
            return gt[n, y * 2 + h].astype(F32) + gb[n, 0, h].astype(F32) + gb[n, 1, h].astype(F32)

        gu[n] = mine(1 - xh).astype(BF16)
        d = send(gu.at[n], gd.at[n], XH)
        yield
        d.wait_recv()
        total = (mine(xh) + gd[n].astype(F32)) * scale
        rest = total[:, 384:512]
        for q in range(3):
            grad_out[p * 3 + q, :, 0:128] = total[:, q * 128 : q * 128 + 128]
            turned = rest if q == 0 else pltpu.roll(rest, 128 - 32 * q, 1)
            grad_out[p * 3 + q, :, 128:160] = turned[:, 0:32]
        yield

    def step(*work):
        for one in work:
            next(one)

    for raw, full in ((w1r, w1), (w2r, w2)):
        mine_at = pl.ds(pl.multiple_of(dp * DPW, 16), DPW)
        for p in range(3):
            rest = jnp.zeros((DPW, 128), F32)
            lane = lax.broadcasted_iota(jnp.int32, (DPW, 128), 1)
            for q in range(3):
                full[mine_at, p * Q + q * 128 : p * Q + q * 128 + 128] = raw[p * 3 + q, :, 0:128]
                tail = jnp.concatenate(
                    [raw[p * 3 + q, :, 128:160].astype(F32), jnp.zeros((DPW, 96), F32)], axis=1
                )
                rest = rest + (tail if q == 0 else pltpu.roll(tail, 32 * q, 1))
            full[mine_at, p * Q + 384 : p * Q + 512] = rest.astype(BF16)

    barrier = pltpu.get_barrier_semaphore()
    for device in (ZP, ZM, XN, YP, YM, XH, CN):
        pl.semaphore_signal(barrier, inc=1, device_id=device, device_id_type=MESH)
    pl.semaphore_wait(barrier, 7)

    get_img = gather_rows(img, imgf, 0)
    get_w1 = gather_weight(w1)
    get_cot = gather_rows(cot, cotp, W)
    get_w2 = gather_weight(w2)
    step(get_img, get_w1)

    imgf[pl.ds(pl.multiple_of(rows * BAND, 16), BAND)] = img[...]
    cotp[pl.ds(pl.multiple_of(W + rows * BAND, 16), BAND)] = cot[...]
    for buffer in (actp, cotp, hp, pp):
        buffer[0:W] = jnp.zeros((W, buffer.shape[1]), BF16)
        buffer[W + PIX : 2 * W + PIX] = jnp.zeros((W, buffer.shape[1]), BF16)
    for basis, held in ((b1, bs1), (b2, bs2)):
        high, low = split(basis[...])
        held[0:RANK] = high
        held[RANK : 2 * RANK] = low
        held[2 * RANK : 3 * RANK] = high

    for _ in range(3):
        step(get_img, get_w1)
    step(get_cot, get_w2)
    step(get_img, get_w1)

    groups = group_matrix(C, lambda row: row)

    def img_rows(i):
        return imgf[pl.ds(pl.multiple_of(i * 16, 16), 16)].astype(F32)

    total = lax.fori_loop(0, PIX // 16, lambda i, acc: acc + fold8(img_rows(i)), jnp.zeros((8, C), F32))
    center = group_mean(total, groups)
    total = lax.fori_loop(
        0, PIX // 16, lambda i, acc: acc + fold8(jnp.square(img_rows(i) - center)), jnp.zeros((8, C), F32)
    )
    factor = lax.rsqrt(group_mean(total, groups) + EPS)

    def activate_rows(i, carry):
        u = (img_rows(i) - center) * factor
        actp[pl.ds(pl.multiple_of(W + i * 16, 16), 16)] = (u / (1.0 + jnp.exp(-u))).astype(BF16)
        return carry

    step(get_cot, get_w2)
    lax.fori_loop(0, PIX // 16, activate_rows, 0)
    step(get_w1)
    step(get_cot, get_w2)

    MT = 288

    def conv_tiles(source, weight, flip):
        def tile(i, carry):
            sums = None
            for p in range(3):
                first = (2 - p if flip else p) * W
                part = dot(
                    source[pl.ds(pl.multiple_of(first + i * MT, 16), MT)],
                    weight[:, p * Q : p * Q + Q],
                )
                sums = part if sums is None else sums + part
            s[pl.ds(pl.multiple_of(i * MT, 16), MT)] = sums
            return carry

        lax.fori_loop(0, PIX // MT, tile, 0)

    conv_tiles(actp, w1, False)
    step(get_cot, get_w2)

    col = lax.broadcasted_iota(jnp.int32, (W, 128), 0)
    lane = lax.broadcasted_iota(jnp.int32, (W, 128), 1)

    def row_at(h, base=0):
        return pl.ds(pl.multiple_of(base + h * W, 16), W)

    def from_left(v):
        return jnp.where(col >= 1, pltpu.roll(v, 1, 0), 0.0)

    def from_right(v):
        return jnp.where(col <= W - 2, pltpu.roll(v, W - 1, 0), 0.0)

    def col_sum(h, first, last):
        part = s[row_at(h)]
        main = first(part[:, 0:128]) + part[:, 128:256] + last(part[:, 256:384])
        rest = part[:, 384:512]
        rest = first(rest) + pltpu.roll(rest, 96, 1) + pltpu.roll(last(rest), 64, 1)
        return main, jnp.where(lane < 32, rest, 0.0)

    def spread_cols(buffer, h, main, rest, first, last):
        at = row_at(h, W)
        buffer[at, 0:128] = first(main).astype(BF16)
        buffer[at, 128:256] = main.astype(BF16)
        buffer[at, 256:384] = last(main).astype(BF16)
        packed = first(rest) + pltpu.roll(rest, 32, 1) + pltpu.roll(last(rest), 64, 1)
        buffer[at, 384:512] = packed.astype(BF16)

    def sum_x(h, acc):
        main, rest = col_sum(h, from_left, from_right)
        x[row_at(h), 0:128] = main
        x[row_at(h), 128:256] = rest
        return acc + fold8(jnp.concatenate([main, rest], axis=1))

    zero_acc = jnp.zeros((8, 256), F32)
    groups_x = group_matrix(256, lambda row: row)
    real = lax.broadcasted_iota(jnp.int32, (1, 256), 1) < RW
    center_x = group_mean(lax.fori_loop(0, H, sum_x, zero_acc), groups_x)

    def dev_x(h, acc):
        d = jnp.where(real, x[row_at(h)] - center_x, 0.0)
        return acc + fold8(d * d)

    factor_x = lax.rsqrt(group_mean(lax.fori_loop(0, H, dev_x, zero_acc), groups_x) + EPS)

    def hidden_rows(h, carry):
        u = jnp.where(real, (x[row_at(h)] - center_x) * factor_x, 0.0)
        x[row_at(h)] = u
        a = u / (1.0 + jnp.exp(-u))
        hidc[row_at(h)] = a.astype(BF16)
        spread_cols(hp, h, a[:, 0:128], a[:, 128:256], from_left, from_right)
        return carry

    lax.fori_loop(0, H, hidden_rows, 0)

    HALF = PIX // 2
    coef = dot_nt(hidc[...], bs2[0 : 2 * RANK])
    coef = coef[:, 0:RANK] + coef[:, RANK : 2 * RANK]
    hb[...] = jnp.concatenate([coef[0:HALF], coef[HALF:PIX]], axis=1).astype(BF16)
    hc0 = send(hb, hx, XN)
    step(get_cot, get_w2)

    def project_act(i, carry):
        a = actp[pl.ds(pl.multiple_of(W + i * 128, 16), 128)]
        c = dot_nt(a, bs1[0 : 2 * RANK])
        high, low = split(c[:, 0:RANK] + c[:, RANK : 2 * RANK])
        back = dot(jnp.concatenate([high, high, low], axis=1), bs1[...])
        left = (a.astype(F32) - back).astype(BF16)
        act_t[:, pl.ds(pl.multiple_of(i * 128, 128), 128)] = left.T
        return carry

    lax.fori_loop(0, PIX // 128, project_act, 0)

    hc0.wait_recv()
    hpair[z] = (hb[...].astype(F32) + hx[...].astype(F32)).astype(BF16)
    hcp = send(hpair.at[z], hpair.at[z], ZP)
    hcm = send(hpair.at[z], hpair.at[z], ZM)

    step(get_w2)
    conv_tiles(cotp, w2, True)

    hcp.wait_recv()
    hfp = send(hpair.at[zm, pl.ds(0, 288)], hpair.at[zm, pl.ds(0, 288)], ZP)
    hcm.wait_recv()
    hfm = send(hpair.at[zp, pl.ds(288, 288)], hpair.at[zp, pl.ds(288, 288)], ZM)

    def grad_rows(h, carry):
        acc, acc_u = carry
        main, rest = col_sum(h, from_right, from_left)
        hg = jnp.concatenate([main, rest], axis=1)
        u = x[row_at(h)]
        sig = 1.0 / (1.0 + jnp.exp(-u))
        d = hg * (sig * (1.0 + u * (1.0 - sig)))
        du[row_at(h)] = d
        return acc + fold8(d), acc_u + fold8(d * u)

    acc, acc_u = lax.fori_loop(0, H, grad_rows, (zero_acc, zero_acc))
    mean_d, mean_du = group_mean(acc, groups_x), group_mean(acc_u, groups_x)

    def pre_rows(h, carry):
        pre = factor_x * (du[row_at(h)] - mean_d - x[row_at(h)] * mean_du)
        pre = jnp.where(real, pre, 0.0)
        spread_cols(pp, h, pre[:, 0:128], pre[:, 128:256], from_right, from_left)
        return carry

    lax.fori_loop(0, H, pre_rows, 0)

    GT = 640

    def grad_tiles(n, left_t, buffer, first):
        def tile(i, carry):
            part = dot(left_t[pl.ds(pl.multiple_of(i * GT, 16), GT)], buffer[first : first + PIX])
            per = GT // (2 * DPW)
            gr[n, pl.ds(i * per, per)] = part.astype(BF16).reshape(per, 2, DPW, Q)
            return carry

        lax.fori_loop(0, C // GT, tile, 0)

    active = []

    def push(new=None):
        for one in list(active):
            if next(one, "done") == "done":
                active.remove(one)
        if new is not None:
            next(new)
            active.append(new)

    for p in range(3):
        grad_tiles(p, act_t, pp, (2 - p) * W)
        push(scatter_grad(p, g1, p))

    def conv_second(zz):
        sums = None
        for p in range(3):
            part = dot_nt(hp[pl.ds(pl.multiple_of(p * W + zz * 288, 16), 288)], w2[:, p * Q : p * Q + Q])
            sums = part if sums is None else sums + part
        o[zz] = sums.astype(BF16).reshape(2, BAND, C)

    def add_into(target, extra):
        return (target.astype(F32) + extra.astype(F32)).astype(BF16)

    conv_second(z2)
    oap, oam = send(o.at[z2, 0], qa.at[0], ZP), send(o.at[z2, 1], qa.at[1], ZM)
    push()
    conv_second(zp)
    conv_second(zm)
    push()
    oap.wait_recv()
    o[zp, 0] = add_into(o[zp, 0], qa[0])
    obp = send(o.at[zp], qb.at[0], ZP)
    oam.wait_recv()
    o[zm, 1] = add_into(o[zm, 1], qa[1])
    obm = send(o.at[zm], qb.at[1], ZM)
    conv_second(z)

    hfp.wait_recv()
    hfm.wait_recv()
    push()

    def project_hidden(h, carry):
        part = hpair[0, row_at(h)].astype(F32)
        for zz in range(1, 4):
            part = part + hpair[zz, row_at(h)].astype(F32)
        for side in range(2):
            high, low = split(part[:, side * RANK : side * RANK + RANK])
            back = dot(jnp.concatenate([high, high, low], axis=1), bs2[...])
            hh = h + side * (H // 2)
            left = hidc[row_at(hh)].astype(F32) - back
            spread_cols(pp, hh, left[:, 0:128], left[:, 128:256], from_left, from_right)
        return carry

    lax.fori_loop(0, H // 2, project_hidden, 0)

    def turn_cot(i, carry):
        cot_t[:, pl.ds(pl.multiple_of(i * 128, 128), 128)] = cotp[
            pl.ds(pl.multiple_of(W + i * 128, 16), 128)
        ].T
        return carry

    lax.fori_loop(0, PIX // 128, turn_cot, 0)

    def band(xx):
        return o[z, xx].astype(F32) + qb[0, xx].astype(F32) + qb[1, xx].astype(F32)

    odx = None
    for p in range(3):
        grad_tiles(3 + p, cot_t, pp, p * W)
        push(scatter_grad(3 + p, g2, p))
        if p == 1:
            obp.wait_recv()
            obm.wait_recv()
            qv[...] = band(1 - xl).astype(BF16)
            odx = send(qv, qd, XN)
    push()
    push()
    odx.wait_recv()
    out[...] = (img[...].astype(F32) + (band(xl) + qd[...].astype(F32))).astype(BF16)
    while active:
        push()
    for copy in pending:
        copy.wait_send()


def body(images, cotangent, first_weight, second_weight, first_basis, second_basis):
    mine = lax.dynamic_slice_in_dim(second_basis, lax.axis_index("rows") * RW, RW, 1)
    mine = jnp.pad(mine, ((0, 0), (0, 256 - RW)))
    vmem = lambda shape, kind=BF16: pltpu.VMEM(shape, kind)
    out, grad_one, grad_two = pl.pallas_call(
        kernel,
        out_shape=(
            jax.ShapeDtypeStruct((BAND, C), BF16),
            jax.ShapeDtypeStruct((9, DPW, RW), F32),
            jax.ShapeDtypeStruct((9, DPW, RW), F32),
        ),
        in_specs=[pl.BlockSpec(memory_space=pltpu.VMEM)] * 6,
        out_specs=[pl.BlockSpec(memory_space=pltpu.VMEM)] * 3,
        scratch_shapes=[
            vmem((PIX, C)),
            vmem((PIX + 2 * W, C)),
            vmem((C, K3)),
            vmem((C, K3)),
            vmem((PIX + 2 * W, C)),
            vmem((PIX, 256), F32),
            vmem((PIX, Q), F32),
            vmem((PIX, 256), F32),
            vmem((PIX, 256)),
            vmem((PIX + 2 * W, Q)),
            vmem((PIX + 2 * W, Q)),
            vmem((C, PIX)),
            vmem((C, PIX)),
            vmem((4, 2, BAND, C)),
            vmem((2, BAND, C)),
            vmem((2, 2, BAND, C)),
            vmem((BAND, C)),
            vmem((BAND, C)),
            vmem((PIX // 2, 128)),
            vmem((PIX // 2, 128)),
            vmem((4, PIX // 2, 128)),
            vmem((6, 8, 2, DPW, Q)),
            vmem((6, 8, DPW, Q)),
            vmem((6, 8, DPW, Q)),
            vmem((6, 2, DPW, Q)),
            vmem((6, 2, 2, DPW, Q)),
            vmem((6, DPW, Q)),
            vmem((6, DPW, Q)),
            vmem((3 * RANK, C)),
            vmem((3 * RANK, 256)),
            pltpu.SemaphoreType.DMA((N_SEM,)),
            pltpu.SemaphoreType.DMA((N_SEM,)),
        ],
        compiler_params=pltpu.CompilerParams(
            collective_id=0, has_side_effects=True, vmem_limit_bytes=66 * 1000 * 1000
        ),
    )(
        images.reshape(BAND, C),
        cotangent.reshape(BAND, C),
        first_weight.reshape(9, DPW, RW),
        second_weight.reshape(9, DPW, RW),
        first_basis,
        mine,
    )
    return (
        out.reshape(1, 3, W, C),
        grad_one.reshape(1, 1, 9, DPW * RW),
        grad_two.reshape(1, 1, 9, DPW * RW),
    )


def solution(mesh):
    return jax.shard_map(
        body,
        mesh=mesh,
        in_specs=(
            P("dp", "rows", None, None),
            P("dp", "rows", None, None),
            P("dp", "rows", None, None),
            P("dp", "rows", None, None),
            P(),
            P(),
        ),
        out_specs=(
            P("dp", "rows", None, None),
            P("dp", "rows", None, None),
            P("dp", "rows", None, None),
        ),
        check_vma=False,
    )
```

```python
import math

import jax
import jax.numpy as jnp
from jax import lax
from jax.experimental import pallas as pl
from jax.experimental.pallas import tpu as pltpu
from jax.sharding import PartitionSpec as P

C = 1280
GSIZE = 40
W = 48
H = 24
PIX = W * H
BAND = 144
DPW = 80
RW = 160
Q = 512
K3 = 3 * Q
RANK = 64
EPS = 1e-05
F32 = jnp.float32
BF16 = jnp.bfloat16
MESH = pl.DeviceIdType.MESH
HIGH = lax.Precision.HIGHEST
N_SEM = 120
PART = 96
AT = 384


def dot(a, b):
    return jnp.dot(a, b, preferred_element_type=F32)


def dot_nt(a, b):
    return lax.dot_general(a, b, (((1,), (1,)), ((), ())), preferred_element_type=F32)


def group_matrix(rows, channel_of):
    channel = channel_of(lax.broadcasted_iota(jnp.int32, (rows, 128), 0))
    group = lax.broadcasted_iota(jnp.int32, (rows, 128), 1) * GSIZE
    return jnp.where((channel >= group) & (channel < group + GSIZE), 1.0, 0.0).astype(F32)


def group_mean(sums, groups):
    per_group = jnp.sum(jnp.dot(sums, groups, precision=HIGH, preferred_element_type=F32), axis=0, keepdims=True)
    spread = lax.dot_general(
        jnp.broadcast_to(per_group, (8, 128)), groups, (((1,), (1,)), ((), ())),
        precision=HIGH, preferred_element_type=F32,
    )
    return spread[0:1] * (1.0 / (PIX * GSIZE))


def fold8(values):
    total = values[0:8]
    for at in range(8, values.shape[0], 8):
        total = total + values[at : at + 8]
    return total


def split(values):
    high = values.astype(BF16)
    low = (values - high.astype(F32)).astype(BF16)
    return high, low


def kernel(
    img, cot, w1r, w2r, b1, b2, out, g1, g2,
    imgf, cotp, w1, w2, actp, x, s, du, hidc, hp, pp, act_t, cot_t,
    o, qa, qb, qd, qv, hb, hx, hpair, gr, gc, gt, ga, gb, gd, gu, bs1, bs2, means, squares,
    ssem, rsem,
):
    dp = lax.axis_index("dp")
    rows = lax.axis_index("rows")
    core = lax.rem(dp, 2)
    xh = lax.rem(dp // 2, 2)
    y = dp // 4
    xl = lax.rem(rows, 2)
    z = rows // 2
    zp, zm, z2 = lax.rem(z + 1, 4), lax.rem(z + 3, 4), lax.rem(z + 2, 4)
    yp, ym, y2 = lax.rem(y + 1, 4), lax.rem(y + 3, 4), lax.rem(y + 2, 4)
    ZP, ZM = (dp, zp * 2 + xl), (dp, zm * 2 + xl)
    XN = (dp, z * 2 + 1 - xl)
    YP, YM = (yp * 4 + xh * 2 + core, rows), (ym * 4 + xh * 2 + core, rows)
    XH = (y * 4 + (1 - xh) * 2 + core, rows)
    CN = (y * 4 + xh * 2 + 1 - core, rows)
    pending = []

    def send(src, dst, device):
        at = len(pending)
        copy = pltpu.make_async_remote_copy(
            src_ref=src, dst_ref=dst, send_sem=ssem.at[at], recv_sem=rsem.at[at],
            device_id=device, device_id_type=MESH,
        )
        copy.start()
        pending.append(copy)
        return copy

    def pass_on(piece, device):
        return send(piece, piece, device)

    def gather_rows(src, full, base):
        one, two = (0, 80), (80, 64)

        def at(zz, xx, part):
            return full.at[pl.ds(pl.multiple_of(base + (zz * 2 + xx) * BAND + part[0], 16), part[1])]

        def own(part, device):
            return send(src.at[pl.ds(part[0], part[1])], at(z, xl, part), device)

        cx = own(one, XN), own(two, XN)
        yield
        cp1, cm2, cp2, cm1 = own(one, ZP), own(two, ZM), own(two, ZP), own(one, ZM)
        yield
        cp1.wait_recv()
        fp = pass_on(at(zm, xl, one), ZP)
        cm2.wait_recv()
        fm = pass_on(at(zp, xl, two), ZM)
        yield
        cx[0].wait_recv()
        ep1, em1 = pass_on(at(z, 1 - xl, one), ZP), pass_on(at(z, 1 - xl, one), ZM)
        yield
        cx[1].wait_recv()
        ep2, em2 = pass_on(at(z, 1 - xl, two), ZP), pass_on(at(z, 1 - xl, two), ZM)
        yield
        cp2.wait_recv()
        cm1.wait_recv()
        yield
        ep1.wait_recv()
        hp_ = pass_on(at(zm, 1 - xl, one), ZP)
        em2.wait_recv()
        hm_ = pass_on(at(zp, 1 - xl, two), ZM)
        yield
        for copy in (fp, fm, ep2, em1):
            copy.wait_recv()
        yield
        hp_.wait_recv()
        hm_.wait_recv()
        yield

    def gather_weight(full):
        one, two, both = (0, 48), (48, 32), (0, DPW)

        def at(yy, hh, part=both):
            return full.at[pl.ds(pl.multiple_of(((yy * 2 + hh) * 2 + core) * DPW + part[0], 16), part[1])]

        last = []

        def to_core(yy, hh):
            last.append(pass_on(at(yy, hh), CN))

        ax = pass_on(at(y, xh, one), XH), pass_on(at(y, xh, two), XH)
        yield
        ap1, am2 = pass_on(at(y, xh, one), YP), pass_on(at(y, xh, two), YM)
        ap2, am1 = pass_on(at(y, xh, two), YP), pass_on(at(y, xh, one), YM)
        to_core(y, xh)
        yield
        ap1.wait_recv()
        fp = pass_on(at(ym, xh, one), YP)
        am2.wait_recv()
        fm = pass_on(at(yp, xh, two), YM)
        yield
        ax[0].wait_recv()
        bp1, bm1 = pass_on(at(y, 1 - xh, one), YP), pass_on(at(y, 1 - xh, one), YM)
        ax[1].wait_recv()
        bp2, bm2 = pass_on(at(y, 1 - xh, two), YP), pass_on(at(y, 1 - xh, two), YM)
        to_core(y, 1 - xh)
        yield
        ap2.wait_recv()
        to_core(ym, xh)
        am1.wait_recv()
        to_core(yp, xh)
        yield
        bp1.wait_recv()
        hp_ = pass_on(at(ym, 1 - xh, one), YP)
        bm2.wait_recv()
        hm_ = pass_on(at(yp, 1 - xh, two), YM)
        yield
        bp2.wait_recv()
        to_core(ym, 1 - xh)
        bm1.wait_recv()
        to_core(yp, 1 - xh)
        fp.wait_recv()
        fm.wait_recv()
        to_core(y2, xh)
        yield
        hp_.wait_recv()
        hm_.wait_recv()
        to_core(y2, 1 - xh)
        yield
        for copy in last:
            copy.wait_recv()
        yield

    scale = 1.0 / math.sqrt(16 * PIX)

    def scatter_grad(n, grad_out, p):
        c = send(gr.at[n, :, 1 - core], gc.at[n], CN)
        yield
        c.wait_recv()
        for block in range(8):
            gt[n, block] = (gr[n, block, core].astype(F32) + gc[n, block].astype(F32)).astype(BF16)
        ap = send(gt.at[n, y2 * 2], ga.at[n, 0], YP)
        am = send(gt.at[n, y2 * 2 + 1], ga.at[n, 1], YM)
        yield
        ap.wait_recv()
        gt[n, yp * 2] = (gt[n, yp * 2].astype(F32) + ga[n, 0].astype(F32)).astype(BF16)
        bp = send(gt.at[n, pl.ds(yp * 2, 2)], gb.at[n, 0], YP)
        am.wait_recv()
        gt[n, ym * 2 + 1] = (gt[n, ym * 2 + 1].astype(F32) + ga[n, 1].astype(F32)).astype(BF16)
        bm = send(gt.at[n, pl.ds(ym * 2, 2)], gb.at[n, 1], YM)
        yield
        bp.wait_recv()
        bm.wait_recv()

        def mine(h):
            return gt[n, y * 2 + h].astype(F32) + gb[n, 0, h].astype(F32) + gb[n, 1, h].astype(F32)

        gu[n] = mine(1 - xh).astype(BF16)
        d = send(gu.at[n], gd.at[n], XH)
        yield
        d.wait_recv()
        total = (mine(xh) + gd[n].astype(F32)) * scale
        rest = total[:, 384:512]
        for q in range(3):
            grad_out[p * 3 + q, :, 0:128] = total[:, q * 128 : q * 128 + 128]
            turned = rest if q == 0 else pltpu.roll(rest, 128 - 32 * q, 1)
            grad_out[p * 3 + q, :, 128:160] = turned[:, 0:32]
        yield

    def step(*work):
        for one in work:
            next(one)

    barrier = pltpu.get_barrier_semaphore()
    for device in (ZP, ZM, XN, YP, YM, XH, CN):
        pl.semaphore_signal(barrier, inc=1, device_id=device, device_id_type=MESH)

    for raw, full in ((w1r, w1), (w2r, w2)):
        mine_at = pl.ds(pl.multiple_of(dp * DPW, 16), DPW)
        for p in range(3):
            rest = jnp.zeros((DPW, 128), F32)
            lane = lax.broadcasted_iota(jnp.int32, (DPW, 128), 1)
            for q in range(3):
                full[mine_at, p * Q + q * 128 : p * Q + q * 128 + 128] = raw[p * 3 + q, :, 0:128]
                tail = jnp.concatenate(
                    [raw[p * 3 + q, :, 128:160].astype(F32), jnp.zeros((DPW, 96), F32)], axis=1
                )
                rest = rest + (tail if q == 0 else pltpu.roll(tail, 32 * q, 1))
            full[mine_at, p * Q + 384 : p * Q + 512] = rest.astype(BF16)

    pl.semaphore_wait(barrier, 7)

    get_img = gather_rows(img, imgf, 0)
    get_w1 = gather_weight(w1)
    get_cot = gather_rows(cot, cotp, W)
    get_w2 = gather_weight(w2)
    step(get_w1, get_img, get_img, get_w1, get_w2, get_cot)

    imgf[pl.ds(pl.multiple_of(rows * BAND, 16), BAND)] = img[...]
    cotp[pl.ds(pl.multiple_of(W + rows * BAND, 16), BAND)] = cot[...]
    for buffer in (actp, cotp, hp, pp):
        buffer[0:W] = jnp.zeros((W, buffer.shape[1]), BF16)
        buffer[W + PIX : 2 * W + PIX] = jnp.zeros((W, buffer.shape[1]), BF16)
    for basis, held in ((b1, bs1), (b2, bs2)):
        high, low = split(basis[...])
        held[0:RANK] = high
        held[RANK : 2 * RANK] = low
        held[2 * RANK : 3 * RANK] = high

    def band_stats(slot, zz, xx):
        base = (zz * 2 + xx) * BAND

        def rows_of(i):
            return imgf[pl.ds(pl.multiple_of(base + i * 16, 16), 16)].astype(F32)

        total = lax.fori_loop(0, BAND // 16, lambda i, acc: acc + fold8(rows_of(i)), jnp.zeros((8, C), F32))
        mean = jnp.sum(total, axis=0, keepdims=True) * (1.0 / BAND)
        means[slot : slot + 1] = mean
        squares[...] = lax.fori_loop(
            0, BAND // 16, lambda i, acc: acc + fold8(jnp.square(rows_of(i) - mean)), squares[...]
        )

    squares[...] = jnp.zeros((8, C), F32)
    band_stats(0, z, xl)
    step(get_w1, get_img, get_w1, get_img, get_img)
    band_stats(1, z, 1 - xl)
    step(get_w1, get_w1, get_img)
    step(get_w2)
    band_stats(2, zm, xl)
    band_stats(3, zp, xl)
    step(get_img, get_cot)
    step(get_w1, get_w1)
    step(get_img)
    band_stats(4, z2, xl)
    band_stats(5, zm, 1 - xl)
    band_stats(6, zp, 1 - xl)
    step(get_w2, get_w2)
    step(get_img)
    band_stats(7, z2, 1 - xl)

    groups = group_matrix(C, lambda row: row)
    center = group_mean(means[...] * BAND, groups)
    total = squares[...] + BAND * jnp.square(means[...] - center)
    factor = lax.rsqrt(group_mean(total, groups) + EPS)

    def img_rows(i):
        return imgf[pl.ds(pl.multiple_of(i * 16, 16), 16)].astype(F32)

    def activate_rows(i, carry):
        u = (img_rows(i) - center) * factor
        actp[pl.ds(pl.multiple_of(W + i * 16, 16), 16)] = (u / (1.0 + jnp.exp(-u))).astype(BF16)
        return carry

    lax.fori_loop(0, PIX // 16, activate_rows, 0)
    step(get_cot, get_cot, get_cot, get_w2, get_w2)
    step(get_w1)

    MT = 288

    def conv_tiles(source, weight, flip, begin=0, end=PIX // MT):
        def tile(i, carry):
            sums = None
            for p in range(3):
                first = (2 - p if flip else p) * W
                part = dot(
                    source[pl.ds(pl.multiple_of(first + i * MT, 16), MT)],
                    weight[:, p * Q : p * Q + Q],
                )
                sums = part if sums is None else sums + part
            s[pl.ds(pl.multiple_of(i * MT, 16), MT)] = sums
            return carry

        lax.fori_loop(begin, end, tile, 0)

    conv_tiles(actp, w1, False)
    step(get_w2, get_cot, get_w2)

    col = lax.broadcasted_iota(jnp.int32, (PART // W, W, 128), 1).reshape(PART, 128)
    lane = lax.broadcasted_iota(jnp.int32, (PART, 128), 1)

    def row_at(h, base=0):
        return pl.ds(pl.multiple_of(base + h * PART, 16), PART)

    def from_left(v):
        return jnp.where(col >= 1, pltpu.roll(v, 1, 0), 0.0)

    def from_right(v):
        return jnp.where(col <= W - 2, pltpu.roll(v, PART - 1, 0), 0.0)

    def col_sum(h, first, last):
        part = s[row_at(h)]
        main = first(part[:, 0:128]) + part[:, 128:256] + last(part[:, 256:384])
        rest = part[:, 384:512]
        rest = first(rest) + pltpu.roll(rest, 96, 1) + pltpu.roll(last(rest), 64, 1)
        return main, jnp.where(lane < 32, rest, 0.0)

    def spread_cols(buffer, h, main, rest, first, last):
        at = row_at(h, W)
        buffer[at, 0:128] = first(main).astype(BF16)
        buffer[at, 128:256] = main.astype(BF16)
        buffer[at, 256:384] = last(main).astype(BF16)
        packed = first(rest) + pltpu.roll(rest, 32, 1) + pltpu.roll(last(rest), 64, 1)
        buffer[at, 384:512] = packed.astype(BF16)

    def sum_x(h, acc):
        main, rest = col_sum(h, from_left, from_right)
        x[row_at(h), 0:128] = main
        x[row_at(h), 128:256] = rest
        return acc + fold8(jnp.concatenate([main, rest], axis=1))

    zero_acc = jnp.zeros((8, 256), F32)
    groups_x = group_matrix(256, lambda row: row)
    real = lax.broadcasted_iota(jnp.int32, (1, 256), 1) < RW
    center_x = group_mean(lax.fori_loop(0, PIX // PART, sum_x, zero_acc), groups_x)

    def dev_x(h, acc):
        d = jnp.where(real, x[row_at(h)] - center_x, 0.0)
        return acc + fold8(d * d)

    factor_x = lax.rsqrt(group_mean(lax.fori_loop(0, PIX // PART, dev_x, zero_acc), groups_x) + EPS)

    def hidden_rows(h, carry):
        u = jnp.where(real, (x[row_at(h)] - center_x) * factor_x, 0.0)
        x[row_at(h)] = u
        a = u / (1.0 + jnp.exp(-u))
        hidc[row_at(h)] = a.astype(BF16)
        spread_cols(hp, h, a[:, 0:128], a[:, 128:256], from_left, from_right)
        return carry

    lax.fori_loop(0, PIX // PART, hidden_rows, 0)

    HALF = PIX // 2
    coef = dot_nt(hidc[...], bs2[0 : 2 * RANK])
    coef = coef[:, 0:RANK] + coef[:, RANK : 2 * RANK]
    hb[...] = jnp.concatenate([coef[0:HALF], coef[HALF:PIX]], axis=1).astype(BF16)
    hc0 = send(hb, hx, XN)

    def project_act(i, carry):
        a = actp[pl.ds(pl.multiple_of(W + i * AT, 16), AT)]
        c = dot_nt(a, bs1[0 : 2 * RANK])
        high, low = split(c[:, 0:RANK] + c[:, RANK : 2 * RANK])
        back = dot(jnp.concatenate([high, high, low], axis=1), bs1[...])
        left = (a.astype(F32) - back).astype(BF16)
        act_t[:, pl.ds(pl.multiple_of(i * AT, 128), AT)] = left.T
        return carry

    project_act(0, 0)
    hc0.wait_recv()
    hpair[z] = (hb[...].astype(F32) + hx[...].astype(F32)).astype(BF16)
    hcp = send(hpair.at[z], hpair.at[z], ZP)
    hcm = send(hpair.at[z], hpair.at[z], ZM)
    step(get_cot)
    project_act(1, 0)
    project_act(2, 0)

    GT = 640

    def grad_tiles(n, left_t, buffer, first):
        def tile(i, carry):
            part = dot(left_t[pl.ds(pl.multiple_of(i * GT, 16), GT)], buffer[first : first + PIX])
            per = GT // (2 * DPW)
            gr[n, pl.ds(i * per, per)] = part.astype(BF16).reshape(per, 2, DPW, Q)
            return carry

        lax.fori_loop(0, C // GT, tile, 0)

    chunks = [scatter_grad(3 + p, g2, p) for p in range(3)] + [scatter_grad(p, g1, p) for p in range(3)]

    def move(*which):
        for one in which:
            next(chunks[one])

    def conv_second(zz):
        sums = None
        for p in range(3):
            part = dot_nt(hp[pl.ds(pl.multiple_of(p * W + zz * 288, 16), 288)], w2[:, p * Q : p * Q + Q])
            sums = part if sums is None else sums + part
        o[zz] = sums.astype(BF16).reshape(2, BAND, C)

    def add_into(target, extra):
        return (target.astype(F32) + extra.astype(F32)).astype(BF16)

    step(get_w2)
    conv_second(z2)
    hcp.wait_recv()
    hfp = send(hpair.at[zm, pl.ds(0, 288)], hpair.at[zm, pl.ds(0, 288)], ZP)
    hcm.wait_recv()
    hfm = send(hpair.at[zp, pl.ds(288, 288)], hpair.at[zp, pl.ds(288, 288)], ZM)
    oap, oam = send(o.at[z2, 0], qa.at[0], ZP), send(o.at[z2, 1], qa.at[1], ZM)

    conv_second(zp)
    hfp.wait_recv()
    hfm.wait_recv()

    def project_hidden(h, carry):
        part = hpair[0, row_at(h)].astype(F32)
        for zz in range(1, 4):
            part = part + hpair[zz, row_at(h)].astype(F32)
        for side in range(2):
            high, low = split(part[:, side * RANK : side * RANK + RANK])
            back = dot(jnp.concatenate([high, high, low], axis=1), bs2[...])
            hh = h + side * (HALF // PART)
            left = hidc[row_at(hh)].astype(F32) - back
            spread_cols(pp, hh, left[:, 0:128], left[:, 128:256], from_left, from_right)
        return carry

    lax.fori_loop(0, HALF // PART, project_hidden, 0)

    step(get_cot, get_cot)

    def turn_cot(i, carry):
        cot_t[:, pl.ds(pl.multiple_of(i * 128, 128), 128)] = cotp[
            pl.ds(pl.multiple_of(W + i * 128, 16), 128)
        ].T
        return carry

    lax.fori_loop(0, PIX // 128, turn_cot, 0)

    grad_tiles(3, cot_t, pp, 0)
    move(0)
    grad_tiles(4, cot_t, pp, W)
    move(1, 0)
    grad_tiles(5, cot_t, pp, 2 * W)
    move(2, 1)
    conv_second(zm)
    move(2)
    oap.wait_recv()
    o[zp, 0] = add_into(o[zp, 0], qa[0])
    obp = send(o.at[zp], qb.at[0], ZP)
    oam.wait_recv()
    o[zm, 1] = add_into(o[zm, 1], qa[1])
    obm = send(o.at[zm], qb.at[1], ZM)
    move(0)

    conv_tiles(cotp, w2, True, 0, 2)
    move(1)
    conv_tiles(cotp, w2, True, 2, 4)
    move(2)

    def grad_rows(h, carry):
        acc, acc_u = carry
        main, rest = col_sum(h, from_right, from_left)
        hg = jnp.concatenate([main, rest], axis=1)
        u = x[row_at(h)]
        sig = 1.0 / (1.0 + jnp.exp(-u))
        d = hg * (sig * (1.0 + u * (1.0 - sig)))
        du[row_at(h)] = d
        return acc + fold8(d), acc_u + fold8(d * u)

    acc, acc_u = lax.fori_loop(0, PIX // PART, grad_rows, (zero_acc, zero_acc))
    move(0)
    mean_d, mean_du = group_mean(acc, groups_x), group_mean(acc_u, groups_x)

    def pre_rows(h, carry):
        pre = factor_x * (du[row_at(h)] - mean_d - x[row_at(h)] * mean_du)
        pre = jnp.where(real, pre, 0.0)
        spread_cols(pp, h, pre[:, 0:128], pre[:, 128:256], from_right, from_left)
        return carry

    lax.fori_loop(0, PIX // PART, pre_rows, 0)

    move(1)

    def band(xx):
        return o[z, xx].astype(F32) + qb[0, xx].astype(F32) + qb[1, xx].astype(F32)

    grad_tiles(0, act_t, pp, 2 * W)
    move(3)
    grad_tiles(1, act_t, pp, W)
    move(4, 3)
    grad_tiles(2, act_t, pp, 0)
    move(5, 4, 2)
    conv_second(z)
    move(5, 3)
    obp.wait_recv()
    obm.wait_recv()
    qv[...] = band(1 - xl).astype(BF16)
    odx = send(qv, qd, XN)

    move(4, 5, 0, 1, 2, 3, 4, 5)
    odx.wait_recv()
    out[...] = (img[...].astype(F32) + (band(xl) + qd[...].astype(F32))).astype(BF16)
    move(3, 4, 5)
    for copy in pending:
        copy.wait_send()


def body(images, cotangent, first_weight, second_weight, first_basis, second_basis):
    mine = lax.dynamic_slice_in_dim(second_basis, lax.axis_index("rows") * RW, RW, 1)
    mine = jnp.pad(mine, ((0, 0), (0, 256 - RW)))
    vmem = lambda shape, kind=BF16: pltpu.VMEM(shape, kind)
    out, grad_one, grad_two = pl.pallas_call(
        kernel,
        out_shape=(
            jax.ShapeDtypeStruct((BAND, C), BF16),
            jax.ShapeDtypeStruct((9, DPW, RW), F32),
            jax.ShapeDtypeStruct((9, DPW, RW), F32),
        ),
        in_specs=[pl.BlockSpec(memory_space=pltpu.VMEM)] * 6,
        out_specs=[pl.BlockSpec(memory_space=pltpu.VMEM)] * 3,
        scratch_shapes=[
            vmem((PIX, C)),
            vmem((PIX + 2 * W, C)),
            vmem((C, K3)),
            vmem((C, K3)),
            vmem((PIX + 2 * W, C)),
            vmem((PIX, 256), F32),
            vmem((PIX, Q), F32),
            vmem((PIX, 256), F32),
            vmem((PIX, 256)),
            vmem((PIX + 2 * W, Q)),
            vmem((PIX + 2 * W, Q)),
            vmem((C, PIX)),
            vmem((C, PIX)),
            vmem((4, 2, BAND, C)),
            vmem((2, BAND, C)),
            vmem((2, 2, BAND, C)),
            vmem((BAND, C)),
            vmem((BAND, C)),
            vmem((PIX // 2, 128)),
            vmem((PIX // 2, 128)),
            vmem((4, PIX // 2, 128)),
            vmem((6, 8, 2, DPW, Q)),
            vmem((6, 8, DPW, Q)),
            vmem((6, 8, DPW, Q)),
            vmem((6, 2, DPW, Q)),
            vmem((6, 2, 2, DPW, Q)),
            vmem((6, DPW, Q)),
            vmem((6, DPW, Q)),
            vmem((3 * RANK, C)),
            vmem((3 * RANK, 256)),
            vmem((8, C), F32),
            vmem((8, C), F32),
            pltpu.SemaphoreType.DMA((N_SEM,)),
            pltpu.SemaphoreType.DMA((N_SEM,)),
        ],
        compiler_params=pltpu.CompilerParams(
            collective_id=0, has_side_effects=True, vmem_limit_bytes=66 * 1000 * 1000
        ),
    )(
        images.reshape(BAND, C),
        cotangent.reshape(BAND, C),
        first_weight.reshape(9, DPW, RW),
        second_weight.reshape(9, DPW, RW),
        first_basis,
        mine,
    )
    return (
        out.reshape(1, 3, W, C),
        grad_one.reshape(1, 1, 9, DPW * RW),
        grad_two.reshape(1, 1, 9, DPW * RW),
    )


def solution(mesh):
    return jax.shard_map(
        body,
        mesh=mesh,
        in_specs=(
            P("dp", "rows", None, None),
            P("dp", "rows", None, None),
            P("dp", "rows", None, None),
            P("dp", "rows", None, None),
            P(),
            P(),
        ),
        out_specs=(
            P("dp", "rows", None, None),
            P("dp", "rows", None, None),
            P("dp", "rows", None, None),
        ),
        check_vma=False,
    )
```

```python
import math

import jax
import jax.numpy as jnp
from jax import lax
from jax.experimental import pallas as pl
from jax.experimental.pallas import tpu as pltpu
from jax.sharding import PartitionSpec as P

C = 1280
GSIZE = 40
W = 48
H = 24
PIX = W * H
BAND = 144
DPW = 80
RW = 160
Q = 512
K3 = 3 * Q
RANK = 64
EPS = 1e-05
F32 = jnp.float32
BF16 = jnp.bfloat16
MESH = pl.DeviceIdType.MESH
HIGH = lax.Precision.HIGHEST
N_SEM = 124
PART = 288
AT = 384


def dot(a, b):
    return jnp.dot(a, b, preferred_element_type=F32)


def dot_nt(a, b):
    return lax.dot_general(a, b, (((1,), (1,)), ((), ())), preferred_element_type=F32)


def group_matrix(rows, channel_of):
    channel = channel_of(lax.broadcasted_iota(jnp.int32, (rows, 128), 0))
    group = lax.broadcasted_iota(jnp.int32, (rows, 128), 1) * GSIZE
    return jnp.where((channel >= group) & (channel < group + GSIZE), 1.0, 0.0).astype(F32)


def group_mean(sums, groups):
    per_group = jnp.sum(jnp.dot(sums, groups, precision=HIGH, preferred_element_type=F32), axis=0, keepdims=True)
    spread = lax.dot_general(
        jnp.broadcast_to(per_group, (8, 128)), groups, (((1,), (1,)), ((), ())),
        precision=HIGH, preferred_element_type=F32,
    )
    return spread[0:1] * (1.0 / (PIX * GSIZE))


def fold8(values):
    total = values[0:8]
    for at in range(8, values.shape[0], 8):
        total = total + values[at : at + 8]
    return total


def split(values):
    high = values.astype(BF16)
    low = (values - high.astype(F32)).astype(BF16)
    return high, low


def kernel(
    img, cot, w1r, w2r, b1, b2, out, g1, g2,
    imgf, cotp, w1, w2, actp, x, s, du, hidc, hp, pp, act_t, cot_t,
    o, qa, qb, qd, qv, hb, hx, hpair, gr, gc, gt, ga, gb, gd, gu, bs1, bs2, means, squares, flat,
    ssem, rsem,
):
    dp = lax.axis_index("dp")
    rows = lax.axis_index("rows")
    core = lax.rem(dp, 2)
    xh = lax.rem(dp // 2, 2)
    y = dp // 4
    xl = lax.rem(rows, 2)
    z = rows // 2
    zp, zm, z2 = lax.rem(z + 1, 4), lax.rem(z + 3, 4), lax.rem(z + 2, 4)
    yp, ym, y2 = lax.rem(y + 1, 4), lax.rem(y + 3, 4), lax.rem(y + 2, 4)
    ZP, ZM = (dp, zp * 2 + xl), (dp, zm * 2 + xl)
    XN = (dp, z * 2 + 1 - xl)
    YP, YM = (yp * 4 + xh * 2 + core, rows), (ym * 4 + xh * 2 + core, rows)
    XH = (y * 4 + (1 - xh) * 2 + core, rows)
    CN = (y * 4 + xh * 2 + 1 - core, rows)
    pending = []

    def send(src, dst, device):
        at = len(pending)
        copy = pltpu.make_async_remote_copy(
            src_ref=src, dst_ref=dst, send_sem=ssem.at[at], recv_sem=rsem.at[at],
            device_id=device, device_id_type=MESH,
        )
        copy.start()
        pending.append(copy)
        return copy

    def pass_on(piece, device):
        return send(piece, piece, device)

    def gather_rows(src, full, base):
        one, two = (0, 80), (80, 64)

        def at(zz, xx, part):
            return full.at[pl.ds(pl.multiple_of(base + (zz * 2 + xx) * BAND + part[0], 16), part[1])]

        def own(part, device):
            return send(src.at[pl.ds(part[0], part[1])], at(z, xl, part), device)

        cx = own(one, XN), own(two, XN)
        yield
        cp1, cm2, cp2, cm1 = own(one, ZP), own(two, ZM), own(two, ZP), own(one, ZM)
        yield
        cp1.wait_recv()
        fp = pass_on(at(zm, xl, one), ZP)
        cm2.wait_recv()
        fm = pass_on(at(zp, xl, two), ZM)
        yield
        cx[0].wait_recv()
        ep1, em1 = pass_on(at(z, 1 - xl, one), ZP), pass_on(at(z, 1 - xl, one), ZM)
        yield
        cx[1].wait_recv()
        ep2, em2 = pass_on(at(z, 1 - xl, two), ZP), pass_on(at(z, 1 - xl, two), ZM)
        yield
        cp2.wait_recv()
        cm1.wait_recv()
        yield
        ep1.wait_recv()
        hp_ = pass_on(at(zm, 1 - xl, one), ZP)
        em2.wait_recv()
        hm_ = pass_on(at(zp, 1 - xl, two), ZM)
        yield
        for copy in (fp, fm, ep2, em1):
            copy.wait_recv()
        yield
        hp_.wait_recv()
        hm_.wait_recv()
        yield

    def gather_rows_late(src, full, base):
        one, two, low, high = (0, 80), (80, 64), (0, 48), (48, 32)

        def at(zz, xx, part):
            return full.at[pl.ds(pl.multiple_of(base + (zz * 2 + xx) * BAND + part[0], 16), part[1])]

        def own(part, device):
            return send(src.at[pl.ds(part[0], part[1])], at(z, xl, part), device)

        cx = own(one, XN), own(two, XN)
        yield
        cp1, cm2, cp2, cm1 = own(one, ZP), own(two, ZM), own(two, ZP), own(one, ZM)
        yield
        cp1.wait_recv()
        fp = pass_on(at(zm, xl, one), ZP)
        cm2.wait_recv()
        fm = pass_on(at(zp, xl, two), ZM)
        gp = pass_on(at(zp, xl, two), XN)
        yield
        cx[0].wait_recv()
        ep, em = pass_on(at(z, 1 - xl, one), ZP), pass_on(at(z, 1 - xl, one), ZM)
        yield
        cp2.wait_recv()
        gm = pass_on(at(zm, xl, two), XN)
        yield
        cx[1].wait_recv()
        cm1.wait_recv()
        yield
        ep.wait_recv()
        hp_ = pass_on(at(zm, 1 - xl, low), ZP)
        em.wait_recv()
        hm_ = pass_on(at(zp, 1 - xl, high), ZM)
        fm.wait_recv()
        gf = pass_on(at(z2, xl, two), XN)
        yield
        for copy in (fp, gp, gm):
            copy.wait_recv()
        yield
        for copy in (hp_, hm_, gf):
            copy.wait_recv()
        yield

    def gather_weight(full):
        one, two, both = (0, 48), (48, 32), (0, DPW)

        def at(yy, hh, part=both):
            return full.at[pl.ds(pl.multiple_of(((yy * 2 + hh) * 2 + core) * DPW + part[0], 16), part[1])]

        last = []

        def to_core(yy, hh):
            last.append(pass_on(at(yy, hh), CN))

        ax = pass_on(at(y, xh, one), XH), pass_on(at(y, xh, two), XH)
        yield
        ap1, am2 = pass_on(at(y, xh, one), YP), pass_on(at(y, xh, two), YM)
        ap2, am1 = pass_on(at(y, xh, two), YP), pass_on(at(y, xh, one), YM)
        to_core(y, xh)
        yield
        ap1.wait_recv()
        fp = pass_on(at(ym, xh, one), YP)
        am2.wait_recv()
        fm = pass_on(at(yp, xh, two), YM)
        yield
        ax[0].wait_recv()
        bp1, bm1 = pass_on(at(y, 1 - xh, one), YP), pass_on(at(y, 1 - xh, one), YM)
        ax[1].wait_recv()
        bp2, bm2 = pass_on(at(y, 1 - xh, two), YP), pass_on(at(y, 1 - xh, two), YM)
        to_core(y, 1 - xh)
        yield
        ap2.wait_recv()
        to_core(ym, xh)
        am1.wait_recv()
        to_core(yp, xh)
        yield
        bp1.wait_recv()
        hp_ = pass_on(at(ym, 1 - xh, one), YP)
        bm2.wait_recv()
        hm_ = pass_on(at(yp, 1 - xh, two), YM)
        yield
        bp2.wait_recv()
        to_core(ym, 1 - xh)
        bm1.wait_recv()
        to_core(yp, 1 - xh)
        fp.wait_recv()
        fm.wait_recv()
        to_core(y2, xh)
        yield
        hp_.wait_recv()
        hm_.wait_recv()
        to_core(y2, 1 - xh)
        yield
        for copy in last:
            copy.wait_recv()
        yield

    scale = 1.0 / math.sqrt(16 * PIX)
    lane20 = lax.broadcasted_iota(jnp.int32, (20, 128), 1)

    def scatter_grad(n, grad_out, p):
        c = send(gr.at[n, :, 1 - core], gc.at[n], CN)
        yield
        c.wait_recv()
        for block in range(8):
            gt[n, block] = (gr[n, block, core].astype(F32) + gc[n, block].astype(F32)).astype(BF16)
        ap = send(gt.at[n, y2 * 2], ga.at[n, 0], YP)
        am = send(gt.at[n, y2 * 2 + 1], ga.at[n, 1], YM)
        yield
        ap.wait_recv()
        gt[n, yp * 2] = (gt[n, yp * 2].astype(F32) + ga[n, 0].astype(F32)).astype(BF16)
        bp = send(gt.at[n, pl.ds(yp * 2, 2)], gb.at[n, 0], YP)
        am.wait_recv()
        gt[n, ym * 2 + 1] = (gt[n, ym * 2 + 1].astype(F32) + ga[n, 1].astype(F32)).astype(BF16)
        bm = send(gt.at[n, pl.ds(ym * 2, 2)], gb.at[n, 1], YM)
        yield
        bp.wait_recv()
        bm.wait_recv()

        def mine(h):
            return gt[n, y * 2 + h].astype(F32) + gb[n, 0, h].astype(F32) + gb[n, 1, h].astype(F32)

        gu[n] = mine(1 - xh).astype(BF16)
        d = send(gu.at[n], gd.at[n], XH)
        yield
        d.wait_recv()
        total = (mine(xh) + gd[n].astype(F32)) * scale
        rest = total[:, 384:512]
        for q in range(3):
            turned = rest if q == 0 else pltpu.roll(rest, 128 - 32 * q, 1)
            flat[0] = total[:, q * 128 : q * 128 + 128]
            flat[1] = turned
            main = [flat[0, pl.ds(i, 20, stride=4)] for i in range(4)]
            tail = [flat[1, pl.ds(i, 20, stride=4)] for i in range(4)]
            pieces = [main[0]]
            for i in range(1, 4):
                shifted = pltpu.roll(main[i], 32 * i, 1)
                low = pltpu.roll(tail[i - 1], 32 * (i - 1), 1)
                low = jnp.where(lane20 < 32 * (i - 1), carried, low) if i > 1 else low
                pieces.append(jnp.where(lane20 < 32 * i, low, shifted))
                carried = shifted
            pieces.append(jnp.where(lane20 < 96, carried, pltpu.roll(tail[3], 96, 1)))
            for j in range(5):
                grad_out[pl.ds((p * 3 + q) * 100 + j, 20, stride=5)] = pieces[j]
        yield

    def step(*work):
        for one in work:
            next(one)

    barrier = pltpu.get_barrier_semaphore()
    for device in (ZP, ZM, XN, YP, YM, XH, CN):
        pl.semaphore_signal(barrier, inc=1, device_id=device, device_id_type=MESH)

    for raw, full in ((w1r, w1), (w2r, w2)):
        mine_at = pl.ds(pl.multiple_of(dp * DPW, 16), DPW)
        for p in range(3):
            rest = jnp.zeros((DPW, 128), F32)
            lane = lax.broadcasted_iota(jnp.int32, (DPW, 128), 1)
            for q in range(3):
                full[mine_at, p * Q + q * 128 : p * Q + q * 128 + 128] = raw[p * 3 + q, :, 0:128]
                tail = jnp.concatenate(
                    [raw[p * 3 + q, :, 128:160].astype(F32), jnp.zeros((DPW, 96), F32)], axis=1
                )
                rest = rest + (tail if q == 0 else pltpu.roll(tail, 32 * q, 1))
            full[mine_at, p * Q + 384 : p * Q + 512] = rest.astype(BF16)

    pl.semaphore_wait(barrier, 7)

    get_img = gather_rows(img, imgf, 0)
    get_w1 = gather_weight(w1)
    get_cot = gather_rows_late(cot, cotp, W)
    get_w2 = gather_weight(w2)
    step(get_w1, get_img, get_img, get_w1, get_w2, get_cot)

    imgf[pl.ds(pl.multiple_of(rows * BAND, 16), BAND)] = img[...]
    cotp[pl.ds(pl.multiple_of(W + rows * BAND, 16), BAND)] = cot[...]
    for buffer in (actp, cotp, hp, pp):
        buffer[0:W] = jnp.zeros((W, buffer.shape[1]), BF16)
        buffer[W + PIX : 2 * W + PIX] = jnp.zeros((W, buffer.shape[1]), BF16)
    for basis, held in ((b1, bs1), (b2, bs2)):
        high, low = split(basis[...])
        held[0:RANK] = high
        held[RANK : 2 * RANK] = low
        held[2 * RANK : 3 * RANK] = high

    def band_stats(slot, zz, xx):
        base = (zz * 2 + xx) * BAND

        def rows_of(i):
            return imgf[pl.ds(pl.multiple_of(base + i * 16, 16), 16)].astype(F32)

        total = lax.fori_loop(0, BAND // 16, lambda i, acc: acc + fold8(rows_of(i)), jnp.zeros((8, C), F32))
        mean = jnp.sum(total, axis=0, keepdims=True) * (1.0 / BAND)
        means[slot : slot + 1] = mean
        squares[...] = lax.fori_loop(
            0, BAND // 16, lambda i, acc: acc + fold8(jnp.square(rows_of(i) - mean)), squares[...]
        )

    squares[...] = jnp.zeros((8, C), F32)
    band_stats(0, z, xl)
    step(get_w1, get_img, get_w1, get_img, get_img)
    band_stats(1, z, 1 - xl)
    step(get_w1, get_w1, get_img)
    step(get_w2)
    band_stats(2, zm, xl)
    band_stats(3, zp, xl)
    step(get_img, get_cot)
    step(get_w1, get_w1)
    step(get_img)
    band_stats(4, z2, xl)
    band_stats(5, zm, 1 - xl)
    band_stats(6, zp, 1 - xl)
    step(get_w2, get_w2)
    step(get_img)
    band_stats(7, z2, 1 - xl)

    groups = group_matrix(C, lambda row: row)
    center = group_mean(means[...] * BAND, groups)
    total = squares[...] + BAND * jnp.square(means[...] - center)
    factor = lax.rsqrt(group_mean(total, groups) + EPS)

    def img_rows(i):
        return imgf[pl.ds(pl.multiple_of(i * 32, 16), 32)].astype(F32)

    def activate_rows(i, carry):
        u = (img_rows(i) - center) * factor
        actp[pl.ds(pl.multiple_of(W + i * 32, 16), 32)] = (u / (1.0 + jnp.exp(-u))).astype(BF16)
        return carry

    lax.fori_loop(0, PIX // 32, activate_rows, 0)
    step(get_cot, get_cot, get_cot, get_w2, get_w2)
    step(get_w1)

    MT = 576

    def conv_tiles(source, weight, flip, begin=0, end=PIX // MT):
        def tile(i, carry):
            sums = None
            for p in range(3):
                first = (2 - p if flip else p) * W
                part = dot(
                    source[pl.ds(pl.multiple_of(first + i * MT, 16), MT)],
                    weight[:, p * Q : p * Q + Q],
                )
                sums = part if sums is None else sums + part
            s[pl.ds(pl.multiple_of(i * MT, 16), MT)] = sums
            return carry

        lax.fori_loop(begin, end, tile, 0)

    conv_tiles(actp, w1, False)
    step(get_w2, get_cot, get_w2)

    col = lax.broadcasted_iota(jnp.int32, (PART // W, W, 128), 1).reshape(PART, 128)
    lane = lax.broadcasted_iota(jnp.int32, (PART, 128), 1)

    def row_at(h, base=0):
        return pl.ds(pl.multiple_of(base + h * PART, 16), PART)

    def from_left(v):
        return jnp.where(col >= 1, pltpu.roll(v, 1, 0), 0.0)

    def from_right(v):
        return jnp.where(col <= W - 2, pltpu.roll(v, PART - 1, 0), 0.0)

    def col_sum(h, first, last):
        part = s[row_at(h)]
        main = first(part[:, 0:128]) + part[:, 128:256] + last(part[:, 256:384])
        rest = part[:, 384:512]
        rest = first(rest) + pltpu.roll(rest, 96, 1) + pltpu.roll(last(rest), 64, 1)
        return main, jnp.where(lane < 32, rest, 0.0)

    def spread_cols(buffer, h, main, rest, first, last):
        at = row_at(h, W)
        buffer[at, 0:128] = first(main).astype(BF16)
        buffer[at, 128:256] = main.astype(BF16)
        buffer[at, 256:384] = last(main).astype(BF16)
        packed = first(rest) + pltpu.roll(rest, 32, 1) + pltpu.roll(last(rest), 64, 1)
        buffer[at, 384:512] = packed.astype(BF16)

    def sum_x(h, acc):
        main, rest = col_sum(h, from_left, from_right)
        x[row_at(h), 0:128] = main
        x[row_at(h), 128:256] = rest
        return acc + fold8(jnp.concatenate([main, rest], axis=1))

    zero_acc = jnp.zeros((8, 256), F32)
    groups_x = group_matrix(256, lambda row: row)
    real = lax.broadcasted_iota(jnp.int32, (1, 256), 1) < RW
    center_x = group_mean(lax.fori_loop(0, PIX // PART, sum_x, zero_acc), groups_x)

    def dev_x(h, acc):
        d = jnp.where(real, x[row_at(h)] - center_x, 0.0)
        return acc + fold8(d * d)

    factor_x = lax.rsqrt(group_mean(lax.fori_loop(0, PIX // PART, dev_x, zero_acc), groups_x) + EPS)

    def hidden_rows(h, carry):
        u = jnp.where(real, (x[row_at(h)] - center_x) * factor_x, 0.0)
        x[row_at(h)] = u
        a = u / (1.0 + jnp.exp(-u))
        hidc[row_at(h)] = a.astype(BF16)
        spread_cols(hp, h, a[:, 0:128], a[:, 128:256], from_left, from_right)
        return carry

    lax.fori_loop(0, PIX // PART, hidden_rows, 0)

    HALF = PIX // 2
    coef = dot_nt(hidc[...], bs2[0 : 2 * RANK])
    coef = coef[:, 0:RANK] + coef[:, RANK : 2 * RANK]
    hb[...] = jnp.concatenate([coef[0:HALF], coef[HALF:PIX]], axis=1).astype(BF16)
    step(get_cot)
    hc0 = send(hb, hx, XN)

    def project_act(i, carry):
        a = actp[pl.ds(pl.multiple_of(W + i * AT, 16), AT)]
        c = dot_nt(a, bs1[0 : 2 * RANK])
        high, low = split(c[:, 0:RANK] + c[:, RANK : 2 * RANK])
        back = dot(jnp.concatenate([high, high, low], axis=1), bs1[...])
        left = (a.astype(F32) - back).astype(BF16)
        act_t[:, pl.ds(pl.multiple_of(i * AT, 128), AT)] = left.T
        return carry

    lax.fori_loop(0, PIX // AT, project_act, 0)
    hc0.wait_recv()
    hpair[z] = (hb[...].astype(F32) + hx[...].astype(F32)).astype(BF16)
    hcp = send(hpair.at[z], hpair.at[z], ZP)
    hcm = send(hpair.at[z], hpair.at[z], ZM)

    GT = 1280

    def grad_tiles(n, left_t, buffer, first):
        def tile(i, carry):
            part = dot(left_t[pl.ds(pl.multiple_of(i * GT, 16), GT)], buffer[first : first + PIX])
            per = GT // (2 * DPW)
            gr[n, pl.ds(i * per, per)] = part.astype(BF16).reshape(per, 2, DPW, Q)
            return carry

        lax.fori_loop(0, C // GT, tile, 0)

    chunks = [scatter_grad(p, g1, p) for p in range(3)] + [scatter_grad(3 + p, g2, p) for p in range(3)]

    def move(*which):
        for one in which:
            next(chunks[one])

    def conv_second(zz):
        sums = None
        for p in range(3):
            part = dot_nt(hp[pl.ds(pl.multiple_of(p * W + zz * 288, 16), 288)], w2[:, p * Q : p * Q + Q])
            sums = part if sums is None else sums + part
        o[zz] = sums.astype(BF16).reshape(2, BAND, C)

    def add_into(target, extra):
        return (target.astype(F32) + extra.astype(F32)).astype(BF16)

    step(get_w2)
    step(get_cot, get_cot)

    conv_tiles(cotp, w2, True)

    def grad_rows(h, carry):
        acc, acc_u = carry
        main, rest = col_sum(h, from_right, from_left)
        hg = jnp.concatenate([main, rest], axis=1)
        u = x[row_at(h)]
        sig = 1.0 / (1.0 + jnp.exp(-u))
        d = hg * (sig * (1.0 + u * (1.0 - sig)))
        du[row_at(h)] = d
        return acc + fold8(d), acc_u + fold8(d * u)

    acc, acc_u = lax.fori_loop(0, PIX // PART, grad_rows, (zero_acc, zero_acc))
    mean_d, mean_du = group_mean(acc, groups_x), group_mean(acc_u, groups_x)

    def pre_rows(h, carry):
        pre = factor_x * (du[row_at(h)] - mean_d - x[row_at(h)] * mean_du)
        pre = jnp.where(real, pre, 0.0)
        spread_cols(pp, h, pre[:, 0:128], pre[:, 128:256], from_right, from_left)
        return carry

    lax.fori_loop(0, PIX // PART, pre_rows, 0)


    grad_tiles(0, act_t, pp, 2 * W)
    move(0)
    conv_second(z2)
    hcp.wait_recv()
    hfp = send(hpair.at[zm, pl.ds(0, 288)], hpair.at[zm, pl.ds(0, 288)], ZP)
    hcm.wait_recv()
    hfm = send(hpair.at[zp, pl.ds(288, 288)], hpair.at[zp, pl.ds(288, 288)], ZM)
    oap, oam = send(o.at[z2, 0], qa.at[0], ZP), send(o.at[z2, 1], qa.at[1], ZM)
    move(0)
    grad_tiles(1, act_t, pp, W)
    move(1)
    conv_second(zp)
    move(1, 0)
    grad_tiles(2, act_t, pp, 0)
    move(2)
    conv_second(zm)
    move(2)
    oap.wait_recv()
    o[zp, 0] = add_into(o[zp, 0], qa[0])
    obp = send(o.at[zp], qb.at[0], ZP)
    oam.wait_recv()
    o[zm, 1] = add_into(o[zm, 1], qa[1])
    obm = send(o.at[zm], qb.at[1], ZM)
    move(1)

    hfp.wait_recv()
    hfm.wait_recv()

    def project_hidden(h, carry):
        part = hpair[0, row_at(h)].astype(F32)
        for zz in range(1, 4):
            part = part + hpair[zz, row_at(h)].astype(F32)
        for side in range(2):
            high, low = split(part[:, side * RANK : side * RANK + RANK])
            back = dot(jnp.concatenate([high, high, low], axis=1), bs2[...])
            hh = h + side * (HALF // PART)
            left = hidc[row_at(hh)].astype(F32) - back
            spread_cols(pp, hh, left[:, 0:128], left[:, 128:256], from_left, from_right)
        return carry

    lax.fori_loop(0, HALF // PART, project_hidden, 0)

    def turn_cot(i, carry):
        cot_t[:, pl.ds(pl.multiple_of(i * 128, 128), 128)] = cotp[
            pl.ds(pl.multiple_of(W + i * 128, 16), 128)
        ].T
        return carry

    lax.fori_loop(0, PIX // 128, turn_cot, 0)

    move(2, 0)
    grad_tiles(3, cot_t, pp, 0)
    move(3)
    conv_second(z)
    move(3, 1)
    grad_tiles(4, cot_t, pp, W)
    move(4, 2, 4)
    grad_tiles(5, cot_t, pp, 2 * W)
    move(5, 3, 5, 4)

    def band(xx):
        return o[z, xx].astype(F32) + qb[0, xx].astype(F32) + qb[1, xx].astype(F32)

    obp.wait_recv()
    obm.wait_recv()
    qv[...] = band(1 - xl).astype(BF16)
    odx = send(qv, qd, XN)
    move(0, 1, 2)
    move(5, 3, 4)
    odx.wait_recv()
    out[...] = (img[...].astype(F32) + (band(xl) + qd[...].astype(F32))).astype(BF16)
    move(5, 3, 4, 5)
    for copy in pending:
        copy.wait_send()


def body(images, cotangent, first_weight, second_weight, first_basis, second_basis):
    mine = lax.dynamic_slice_in_dim(second_basis, lax.axis_index("rows") * RW, RW, 1)
    mine = jnp.pad(mine, ((0, 0), (0, 256 - RW)))
    vmem = lambda shape, kind=BF16: pltpu.VMEM(shape, kind)
    out, grad_one, grad_two = pl.pallas_call(
        kernel,
        out_shape=(
            jax.ShapeDtypeStruct((BAND, C), BF16),
            jax.ShapeDtypeStruct((9 * DPW * RW // 128, 128), F32),
            jax.ShapeDtypeStruct((9 * DPW * RW // 128, 128), F32),
        ),
        in_specs=[pl.BlockSpec(memory_space=pltpu.VMEM)] * 6,
        out_specs=[pl.BlockSpec(memory_space=pltpu.VMEM)] * 3,
        scratch_shapes=[
            vmem((PIX, C)),
            vmem((PIX + 2 * W, C)),
            vmem((C, K3)),
            vmem((C, K3)),
            vmem((PIX + 2 * W, C)),
            vmem((PIX, 256), F32),
            vmem((PIX, Q), F32),
            vmem((PIX, 256), F32),
            vmem((PIX, 256)),
            vmem((PIX + 2 * W, Q)),
            vmem((PIX + 2 * W, Q)),
            vmem((C, PIX)),
            vmem((C, PIX)),
            vmem((4, 2, BAND, C)),
            vmem((2, BAND, C)),
            vmem((2, 2, BAND, C)),
            vmem((BAND, C)),
            vmem((BAND, C)),
            vmem((PIX // 2, 128)),
            vmem((PIX // 2, 128)),
            vmem((4, PIX // 2, 128)),
            vmem((6, 8, 2, DPW, Q)),
            vmem((6, 8, DPW, Q)),
            vmem((6, 8, DPW, Q)),
            vmem((6, 2, DPW, Q)),
            vmem((6, 2, 2, DPW, Q)),
            vmem((6, DPW, Q)),
            vmem((6, DPW, Q)),
            vmem((3 * RANK, C)),
            vmem((3 * RANK, 256)),
            vmem((8, C), F32),
            vmem((8, C), F32),
            vmem((2, DPW, 128), F32),
            pltpu.SemaphoreType.DMA((N_SEM,)),
            pltpu.SemaphoreType.DMA((N_SEM,)),
        ],
        compiler_params=pltpu.CompilerParams(
            collective_id=0, has_side_effects=True, vmem_limit_bytes=66 * 1000 * 1000
        ),
    )(
        images.reshape(BAND, C),
        cotangent.reshape(BAND, C),
        first_weight.reshape(9, DPW, RW),
        second_weight.reshape(9, DPW, RW),
        first_basis,
        mine,
    )
    return (
        out.reshape(1, 3, W, C),
        grad_one.reshape(1, 1, 9, DPW * RW),
        grad_two.reshape(1, 1, 9, DPW * RW),
    )


def solution(mesh):
    return jax.shard_map(
        body,
        mesh=mesh,
        in_specs=(
            P("dp", "rows", None, None),
            P("dp", "rows", None, None),
            P("dp", "rows", None, None),
            P("dp", "rows", None, None),
            P(),
            P(),
        ),
        out_specs=(
            P("dp", "rows", None, None),
            P("dp", "rows", None, None),
            P("dp", "rows", None, None),
        ),
        check_vma=False,
    )
```

```python
import math

import jax
import jax.numpy as jnp
from jax import lax
from jax.experimental import pallas as pl
from jax.experimental.pallas import tpu as pltpu
from jax.sharding import PartitionSpec as P

C = 1280
GSIZE = 40
W = 48
H = 24
PIX = W * H
BAND = 144
DPW = 80
RW = 160
Q = 512
K3 = 3 * Q
RANK = 64
EPS = 1e-05
F32 = jnp.float32
BF16 = jnp.bfloat16
MESH = pl.DeviceIdType.MESH
HIGH = lax.Precision.HIGHEST
N_SEM = 124
PART = 288
AT = 384


def dot(a, b):
    return jnp.dot(a, b, preferred_element_type=F32)


def dot_nt(a, b):
    return lax.dot_general(a, b, (((1,), (1,)), ((), ())), preferred_element_type=F32)


def group_matrix(rows, channel_of):
    channel = channel_of(lax.broadcasted_iota(jnp.int32, (rows, 128), 0))
    group = lax.broadcasted_iota(jnp.int32, (rows, 128), 1) * GSIZE
    return jnp.where((channel >= group) & (channel < group + GSIZE), 1.0, 0.0).astype(F32)


def group_mean(sums, groups):
    per_group = jnp.sum(jnp.dot(sums, groups, precision=HIGH, preferred_element_type=F32), axis=0, keepdims=True)
    spread = lax.dot_general(
        jnp.broadcast_to(per_group, (8, 128)), groups, (((1,), (1,)), ((), ())),
        precision=HIGH, preferred_element_type=F32,
    )
    return spread[0:1] * (1.0 / (PIX * GSIZE))


def fold8(values):
    total = values[0:8]
    for at in range(8, values.shape[0], 8):
        total = total + values[at : at + 8]
    return total


def split(values):
    high = values.astype(BF16)
    low = (values - high.astype(F32)).astype(BF16)
    return high, low


def kernel(
    img, cot, w1r, w2r, b1, b2, out, g1, g2,
    imgf, cotp, w1, w2, actp, x, s, du, hidc, hp, pp, act_t, cot_t,
    o, qa, qb, qd, qv, hb, hx, hpair, gr, gc, gt, ga, gb, gd, gu, bs1, bs2, means, squares, flat,
    ssem, rsem,
):
    dp = lax.axis_index("dp")
    rows = lax.axis_index("rows")
    core = lax.rem(dp, 2)
    xh = lax.rem(dp // 2, 2)
    y = dp // 4
    xl = lax.rem(rows, 2)
    z = rows // 2
    zp, zm, z2 = lax.rem(z + 1, 4), lax.rem(z + 3, 4), lax.rem(z + 2, 4)
    yp, ym, y2 = lax.rem(y + 1, 4), lax.rem(y + 3, 4), lax.rem(y + 2, 4)
    ZP, ZM = (dp, zp * 2 + xl), (dp, zm * 2 + xl)
    XN = (dp, z * 2 + 1 - xl)
    YP, YM = (yp * 4 + xh * 2 + core, rows), (ym * 4 + xh * 2 + core, rows)
    XH = (y * 4 + (1 - xh) * 2 + core, rows)
    CN = (y * 4 + xh * 2 + 1 - core, rows)
    pending = []

    def send(src, dst, device):
        at = len(pending)
        copy = pltpu.make_async_remote_copy(
            src_ref=src, dst_ref=dst, send_sem=ssem.at[at], recv_sem=rsem.at[at],
            device_id=device, device_id_type=MESH,
        )
        copy.start()
        pending.append(copy)
        return copy

    def pass_on(piece, device):
        return send(piece, piece, device)

    def gather_rows(src, full, base):
        one, two = (0, 80), (80, 64)

        def at(zz, xx, part):
            return full.at[pl.ds(pl.multiple_of(base + (zz * 2 + xx) * BAND + part[0], 16), part[1])]

        def own(part, device):
            return send(src.at[pl.ds(part[0], part[1])], at(z, xl, part), device)

        cx = own(one, XN), own(two, XN)
        yield
        cp1, cm2, cp2, cm1 = own(one, ZP), own(two, ZM), own(two, ZP), own(one, ZM)
        yield
        cp1.wait_recv()
        fp = pass_on(at(zm, xl, one), ZP)
        cm2.wait_recv()
        fm = pass_on(at(zp, xl, two), ZM)
        yield
        cx[0].wait_recv()
        ep1, em1 = pass_on(at(z, 1 - xl, one), ZP), pass_on(at(z, 1 - xl, one), ZM)
        yield
        cx[1].wait_recv()
        ep2, em2 = pass_on(at(z, 1 - xl, two), ZP), pass_on(at(z, 1 - xl, two), ZM)
        yield
        cp2.wait_recv()
        cm1.wait_recv()
        yield
        ep1.wait_recv()
        hp_ = pass_on(at(zm, 1 - xl, one), ZP)
        em2.wait_recv()
        hm_ = pass_on(at(zp, 1 - xl, two), ZM)
        yield
        for copy in (fp, fm, ep2, em1):
            copy.wait_recv()
        yield
        hp_.wait_recv()
        hm_.wait_recv()
        yield

    def gather_rows_late(src, full, base):
        one, two, low, high = (0, 80), (80, 64), (0, 48), (48, 32)

        def at(zz, xx, part):
            return full.at[pl.ds(pl.multiple_of(base + (zz * 2 + xx) * BAND + part[0], 16), part[1])]

        def own(part, device):
            return send(src.at[pl.ds(part[0], part[1])], at(z, xl, part), device)

        cx = own(one, XN), own(two, XN)
        yield
        cp1, cm2, cp2, cm1 = own(one, ZP), own(two, ZM), own(two, ZP), own(one, ZM)
        yield
        cp1.wait_recv()
        fp = pass_on(at(zm, xl, one), ZP)
        cm2.wait_recv()
        fm = pass_on(at(zp, xl, two), ZM)
        gp = pass_on(at(zp, xl, two), XN)
        yield
        cx[0].wait_recv()
        ep, em = pass_on(at(z, 1 - xl, one), ZP), pass_on(at(z, 1 - xl, one), ZM)
        yield
        cp2.wait_recv()
        gm = pass_on(at(zm, xl, two), XN)
        yield
        cx[1].wait_recv()
        cm1.wait_recv()
        yield
        ep.wait_recv()
        hp_ = pass_on(at(zm, 1 - xl, low), ZP)
        em.wait_recv()
        hm_ = pass_on(at(zp, 1 - xl, high), ZM)
        fm.wait_recv()
        gf = pass_on(at(z2, xl, two), XN)
        yield
        for copy in (fp, gp, gm):
            copy.wait_recv()
        yield
        for copy in (hp_, hm_, gf):
            copy.wait_recv()
        yield

    def gather_weight(full):
        one, two, both = (0, 48), (48, 32), (0, DPW)

        def at(yy, hh, part=both):
            return full.at[pl.ds(pl.multiple_of(((yy * 2 + hh) * 2 + core) * DPW + part[0], 16), part[1])]

        last = []

        def to_core(yy, hh):
            last.append(pass_on(at(yy, hh), CN))

        ax = pass_on(at(y, xh, one), XH), pass_on(at(y, xh, two), XH)
        yield
        ap1, am2 = pass_on(at(y, xh, one), YP), pass_on(at(y, xh, two), YM)
        ap2, am1 = pass_on(at(y, xh, two), YP), pass_on(at(y, xh, one), YM)
        to_core(y, xh)
        yield
        ap1.wait_recv()
        fp = pass_on(at(ym, xh, one), YP)
        am2.wait_recv()
        fm = pass_on(at(yp, xh, two), YM)
        yield
        ax[0].wait_recv()
        bp1, bm1 = pass_on(at(y, 1 - xh, one), YP), pass_on(at(y, 1 - xh, one), YM)
        ax[1].wait_recv()
        bp2, bm2 = pass_on(at(y, 1 - xh, two), YP), pass_on(at(y, 1 - xh, two), YM)
        to_core(y, 1 - xh)
        yield
        ap2.wait_recv()
        to_core(ym, xh)
        am1.wait_recv()
        to_core(yp, xh)
        yield
        bp1.wait_recv()
        hp_ = pass_on(at(ym, 1 - xh, one), YP)
        bm2.wait_recv()
        hm_ = pass_on(at(yp, 1 - xh, two), YM)
        yield
        bp2.wait_recv()
        to_core(ym, 1 - xh)
        bm1.wait_recv()
        to_core(yp, 1 - xh)
        fp.wait_recv()
        fm.wait_recv()
        to_core(y2, xh)
        yield
        hp_.wait_recv()
        hm_.wait_recv()
        to_core(y2, 1 - xh)
        yield
        for copy in last:
            copy.wait_recv()
        yield

    scale = 1.0 / math.sqrt(16 * PIX)
    lane20 = lax.broadcasted_iota(jnp.int32, (20, 128), 1)

    def scatter_grad(n, grad_out, p):
        c = send(gr.at[n, :, 1 - core], gc.at[n], CN)
        yield
        c.wait_recv()
        for block in range(8):
            gt[n, block] = (gr[n, block, core].astype(F32) + gc[n, block].astype(F32)).astype(BF16)
        ap = send(gt.at[n, y2 * 2], ga.at[n, 0], YP)
        am = send(gt.at[n, y2 * 2 + 1], ga.at[n, 1], YM)
        yield
        ap.wait_recv()
        gt[n, yp * 2] = (gt[n, yp * 2].astype(F32) + ga[n, 0].astype(F32)).astype(BF16)
        bp = send(gt.at[n, pl.ds(yp * 2, 2)], gb.at[n, 0], YP)
        am.wait_recv()
        gt[n, ym * 2 + 1] = (gt[n, ym * 2 + 1].astype(F32) + ga[n, 1].astype(F32)).astype(BF16)
        bm = send(gt.at[n, pl.ds(ym * 2, 2)], gb.at[n, 1], YM)
        yield
        bp.wait_recv()
        bm.wait_recv()

        def mine(h):
            return gt[n, y * 2 + h].astype(F32) + gb[n, 0, h].astype(F32) + gb[n, 1, h].astype(F32)

        gu[n] = mine(1 - xh).astype(BF16)
        d = send(gu.at[n], gd.at[n], XH)
        yield
        d.wait_recv()
        total = (mine(xh) + gd[n].astype(F32)) * scale
        rest = total[:, 384:512]
        for q in range(3):
            turned = rest if q == 0 else pltpu.roll(rest, 128 - 32 * q, 1)
            flat[0] = total[:, q * 128 : q * 128 + 128]
            flat[1] = turned
            main = [flat[0, pl.ds(i, 20, stride=4)] for i in range(4)]
            tail = [flat[1, pl.ds(i, 20, stride=4)] for i in range(4)]
            pieces = [main[0]]
            for i in range(1, 4):
                shifted = pltpu.roll(main[i], 32 * i, 1)
                low = pltpu.roll(tail[i - 1], 32 * (i - 1), 1)
                low = jnp.where(lane20 < 32 * (i - 1), carried, low) if i > 1 else low
                pieces.append(jnp.where(lane20 < 32 * i, low, shifted))
                carried = shifted
            pieces.append(jnp.where(lane20 < 96, carried, pltpu.roll(tail[3], 96, 1)))
            for j in range(5):
                grad_out[pl.ds((p * 3 + q) * 100 + j, 20, stride=5)] = pieces[j]
        yield

    def step(*work):
        for one in work:
            next(one)

    barrier = pltpu.get_barrier_semaphore()
    for device in (ZP, ZM, XN, YP, YM, XH, CN):
        pl.semaphore_signal(barrier, inc=1, device_id=device, device_id_type=MESH)

    for raw, full in ((w1r, w1), (w2r, w2)):
        mine_at = pl.ds(pl.multiple_of(dp * DPW, 16), DPW)
        for p in range(3):
            rest = jnp.zeros((DPW, 128), F32)
            lane = lax.broadcasted_iota(jnp.int32, (DPW, 128), 1)
            for q in range(3):
                full[mine_at, p * Q + q * 128 : p * Q + q * 128 + 128] = raw[p * 3 + q, :, 0:128]
                tail = jnp.concatenate(
                    [raw[p * 3 + q, :, 128:160].astype(F32), jnp.zeros((DPW, 96), F32)], axis=1
                )
                rest = rest + (tail if q == 0 else pltpu.roll(tail, 32 * q, 1))
            full[mine_at, p * Q + 384 : p * Q + 512] = rest.astype(BF16)

    pl.semaphore_wait(barrier, 7)

    get_img = gather_rows(img, imgf, 0)
    get_w1 = gather_weight(w1)
    get_cot = gather_rows_late(cot, cotp, W)
    get_w2 = gather_weight(w2)
    step(get_w1, get_img, get_img, get_w1, get_w2, get_cot)

    imgf[pl.ds(pl.multiple_of(rows * BAND, 16), BAND)] = img[...]
    cotp[pl.ds(pl.multiple_of(W + rows * BAND, 16), BAND)] = cot[...]
    for buffer in (actp, cotp, hp, pp):
        buffer[0:W] = jnp.zeros((W, buffer.shape[1]), BF16)
        buffer[W + PIX : 2 * W + PIX] = jnp.zeros((W, buffer.shape[1]), BF16)
    for basis, held in ((b1, bs1), (b2, bs2)):
        high, low = split(basis[...])
        held[0:RANK] = high
        held[RANK : 2 * RANK] = low
        held[2 * RANK : 3 * RANK] = high

    def band_stats(slot, zz, xx):
        base = (zz * 2 + xx) * BAND

        def rows_of(i):
            return imgf[pl.ds(pl.multiple_of(base + i * 16, 16), 16)].astype(F32)

        total = lax.fori_loop(0, BAND // 16, lambda i, acc: acc + fold8(rows_of(i)), jnp.zeros((8, C), F32))
        mean = jnp.sum(total, axis=0, keepdims=True) * (1.0 / BAND)
        means[slot : slot + 1] = mean
        squares[...] = lax.fori_loop(
            0, BAND // 16, lambda i, acc: acc + fold8(jnp.square(rows_of(i) - mean)), squares[...]
        )

    squares[...] = jnp.zeros((8, C), F32)
    band_stats(0, z, xl)
    step(get_w1, get_img, get_w1, get_img, get_img)
    band_stats(1, z, 1 - xl)
    step(get_w1, get_w1, get_img)
    step(get_w2)
    band_stats(2, zm, xl)
    band_stats(3, zp, xl)
    step(get_img, get_cot)
    step(get_w1, get_w1)
    step(get_img)
    band_stats(4, z2, xl)
    band_stats(5, zm, 1 - xl)
    band_stats(6, zp, 1 - xl)
    step(get_w2, get_w2)
    step(get_img)
    band_stats(7, z2, 1 - xl)

    groups = group_matrix(C, lambda row: row)
    center = group_mean(means[...] * BAND, groups)
    total = squares[...] + BAND * jnp.square(means[...] - center)
    factor = lax.rsqrt(group_mean(total, groups) + EPS)

    def img_rows(i):
        return imgf[pl.ds(pl.multiple_of(i * 32, 16), 32)].astype(F32)

    def activate_rows(i, carry):
        u = (img_rows(i) - center) * factor
        actp[pl.ds(pl.multiple_of(W + i * 32, 16), 32)] = (u / (1.0 + jnp.exp(-u))).astype(BF16)
        return carry

    lax.fori_loop(0, PIX // 32, activate_rows, 0)
    step(get_cot, get_cot, get_w2, get_w2)
    step(get_w1)

    MT = 576

    def conv_tiles(source, weight, flip, begin=0, end=PIX // MT):
        def tile(i, carry):
            sums = None
            for p in range(3):
                first = (2 - p if flip else p) * W
                part = dot(
                    source[pl.ds(pl.multiple_of(first + i * MT, 16), MT)],
                    weight[:, p * Q : p * Q + Q],
                )
                sums = part if sums is None else sums + part
            s[pl.ds(pl.multiple_of(i * MT, 16), MT)] = sums
            return carry

        lax.fori_loop(begin, end, tile, 0)

    conv_tiles(actp, w1, False)
    step(get_w2, get_cot, get_cot, get_w2)

    col = lax.broadcasted_iota(jnp.int32, (PART // W, W, 128), 1).reshape(PART, 128)
    lane = lax.broadcasted_iota(jnp.int32, (PART, 128), 1)

    def row_at(h, base=0):
        return pl.ds(pl.multiple_of(base + h * PART, 16), PART)

    def from_left(v):
        return jnp.where(col >= 1, pltpu.roll(v, 1, 0), 0.0)

    def from_right(v):
        return jnp.where(col <= W - 2, pltpu.roll(v, PART - 1, 0), 0.0)

    def col_sum(h, first, last):
        part = s[row_at(h)]
        main = first(part[:, 0:128]) + part[:, 128:256] + last(part[:, 256:384])
        rest = part[:, 384:512]
        rest = first(rest) + pltpu.roll(rest, 96, 1) + pltpu.roll(last(rest), 64, 1)
        return main, jnp.where(lane < 32, rest, 0.0)

    def spread_cols(buffer, h, main, rest, first, last):
        at = row_at(h, W)
        buffer[at, 0:128] = first(main).astype(BF16)
        buffer[at, 128:256] = main.astype(BF16)
        buffer[at, 256:384] = last(main).astype(BF16)
        packed = first(rest) + pltpu.roll(rest, 32, 1) + pltpu.roll(last(rest), 64, 1)
        buffer[at, 384:512] = packed.astype(BF16)

    def sum_x(h, acc):
        main, rest = col_sum(h, from_left, from_right)
        x[row_at(h), 0:128] = main
        x[row_at(h), 128:256] = rest
        return acc + fold8(jnp.concatenate([main, rest], axis=1))

    zero_acc = jnp.zeros((8, 256), F32)
    groups_x = group_matrix(256, lambda row: row)
    real = lax.broadcasted_iota(jnp.int32, (1, 256), 1) < RW
    center_x = group_mean(lax.fori_loop(0, PIX // PART, sum_x, zero_acc), groups_x)

    def dev_x(h, acc):
        d = jnp.where(real, x[row_at(h)] - center_x, 0.0)
        return acc + fold8(d * d)

    factor_x = lax.rsqrt(group_mean(lax.fori_loop(0, PIX // PART, dev_x, zero_acc), groups_x) + EPS)

    def hidden_rows(h, carry):
        u = jnp.where(real, (x[row_at(h)] - center_x) * factor_x, 0.0)
        x[row_at(h)] = u
        a = u / (1.0 + jnp.exp(-u))
        hidc[row_at(h)] = a.astype(BF16)
        spread_cols(hp, h, a[:, 0:128], a[:, 128:256], from_left, from_right)
        return carry

    lax.fori_loop(0, PIX // PART, hidden_rows, 0)

    HALF = PIX // 2
    coef = dot_nt(hidc[...], bs2[0 : 2 * RANK])
    coef = coef[:, 0:RANK] + coef[:, RANK : 2 * RANK]
    hb[...] = jnp.concatenate([coef[0:HALF], coef[HALF:PIX]], axis=1).astype(BF16)
    step(get_cot)
    hc0 = send(hb, hx, XN)

    def project_act(i, carry):
        a = actp[pl.ds(pl.multiple_of(W + i * AT, 16), AT)]
        c = dot_nt(a, bs1[0 : 2 * RANK])
        high, low = split(c[:, 0:RANK] + c[:, RANK : 2 * RANK])
        back = dot(jnp.concatenate([high, high, low], axis=1), bs1[...])
        left = (a.astype(F32) - back).astype(BF16)
        act_t[:, pl.ds(pl.multiple_of(i * AT, 128), AT)] = left.T
        return carry

    lax.fori_loop(0, PIX // AT, project_act, 0)

    GT = 1280

    def grad_tiles(n, left_t, buffer, first):
        def tile(i, carry):
            part = dot(left_t[pl.ds(pl.multiple_of(i * GT, 16), GT)], buffer[first : first + PIX])
            per = GT // (2 * DPW)
            gr[n, pl.ds(i * per, per)] = part.astype(BF16).reshape(per, 2, DPW, Q)
            return carry

        lax.fori_loop(0, C // GT, tile, 0)

    chunks = [scatter_grad(p, g1, p) for p in range(3)] + [scatter_grad(3 + p, g2, p) for p in range(3)]

    def move(*which):
        for one in which:
            next(chunks[one])

    def conv_second(zz):
        sums = None
        for p in range(3):
            part = dot_nt(hp[pl.ds(pl.multiple_of(p * W + zz * 288, 16), 288)], w2[:, p * Q : p * Q + Q])
            sums = part if sums is None else sums + part
        o[zz] = sums.astype(BF16).reshape(2, BAND, C)

    def add_into(target, extra):
        return (target.astype(F32) + extra.astype(F32)).astype(BF16)

    step(get_w2)
    step(get_cot, get_cot)

    conv_tiles(cotp, w2, True)
    hc0.wait_recv()
    hpair[z] = (hb[...].astype(F32) + hx[...].astype(F32)).astype(BF16)
    hcp = send(hpair.at[z], hpair.at[z], ZP)
    hcm = send(hpair.at[z], hpair.at[z], ZM)

    def grad_rows(h, carry):
        acc, acc_u = carry
        main, rest = col_sum(h, from_right, from_left)
        hg = jnp.concatenate([main, rest], axis=1)
        u = x[row_at(h)]
        sig = 1.0 / (1.0 + jnp.exp(-u))
        d = hg * (sig * (1.0 + u * (1.0 - sig)))
        du[row_at(h)] = d
        return acc + fold8(d), acc_u + fold8(d * u)

    acc, acc_u = lax.fori_loop(0, PIX // PART, grad_rows, (zero_acc, zero_acc))
    mean_d, mean_du = group_mean(acc, groups_x), group_mean(acc_u, groups_x)

    def pre_rows(h, carry):
        pre = factor_x * (du[row_at(h)] - mean_d - x[row_at(h)] * mean_du)
        pre = jnp.where(real, pre, 0.0)
        spread_cols(pp, h, pre[:, 0:128], pre[:, 128:256], from_right, from_left)
        return carry

    lax.fori_loop(0, PIX // PART, pre_rows, 0)


    grad_tiles(0, act_t, pp, 2 * W)
    move(0)
    conv_second(z2)
    hcp.wait_recv()
    hfp = send(hpair.at[zm, pl.ds(0, 288)], hpair.at[zm, pl.ds(0, 288)], ZP)
    hcm.wait_recv()
    hfm = send(hpair.at[zp, pl.ds(288, 288)], hpair.at[zp, pl.ds(288, 288)], ZM)
    oap, oam = send(o.at[z2, 0], qa.at[0], ZP), send(o.at[z2, 1], qa.at[1], ZM)
    move(0)
    grad_tiles(1, act_t, pp, W)
    move(1)
    conv_second(zp)
    move(1, 0)
    grad_tiles(2, act_t, pp, 0)
    move(2)
    conv_second(zm)
    move(2)
    oap.wait_recv()
    o[zp, 0] = add_into(o[zp, 0], qa[0])
    obp = send(o.at[zp], qb.at[0], ZP)
    oam.wait_recv()
    o[zm, 1] = add_into(o[zm, 1], qa[1])
    obm = send(o.at[zm], qb.at[1], ZM)
    move(1)

    hfp.wait_recv()
    hfm.wait_recv()

    def project_hidden(h, carry):
        part = hpair[0, row_at(h)].astype(F32)
        for zz in range(1, 4):
            part = part + hpair[zz, row_at(h)].astype(F32)
        for side in range(2):
            high, low = split(part[:, side * RANK : side * RANK + RANK])
            back = dot(jnp.concatenate([high, high, low], axis=1), bs2[...])
            hh = h + side * (HALF // PART)
            left = hidc[row_at(hh)].astype(F32) - back
            spread_cols(pp, hh, left[:, 0:128], left[:, 128:256], from_left, from_right)
        return carry

    lax.fori_loop(0, HALF // PART, project_hidden, 0)

    def turn_cot(i, carry):
        cot_t[:, pl.ds(pl.multiple_of(i * 128, 128), 128)] = cotp[
            pl.ds(pl.multiple_of(W + i * 128, 16), 128)
        ].T
        return carry

    lax.fori_loop(0, PIX // 128, turn_cot, 0)

    move(2, 0)
    grad_tiles(3, cot_t, pp, 0)
    move(3)
    conv_second(z)
    move(3, 1)
    grad_tiles(4, cot_t, pp, W)
    move(4, 2, 4, 3)
    grad_tiles(5, cot_t, pp, 2 * W)
    move(5, 0, 1, 5, 4)

    def band(xx):
        return o[z, xx].astype(F32) + qb[0, xx].astype(F32) + qb[1, xx].astype(F32)

    obp.wait_recv()
    obm.wait_recv()
    qv[...] = band(1 - xl).astype(BF16)
    odx = send(qv, qd, XN)
    move(2, 3, 5, 4)
    odx.wait_recv()
    out[...] = (img[...].astype(F32) + (band(xl) + qd[...].astype(F32))).astype(BF16)
    move(5, 3, 4, 5)
    for copy in pending:
        copy.wait_send()


def body(images, cotangent, first_weight, second_weight, first_basis, second_basis):
    mine = lax.dynamic_slice_in_dim(second_basis, lax.axis_index("rows") * RW, RW, 1)
    mine = jnp.pad(mine, ((0, 0), (0, 256 - RW)))
    vmem = lambda shape, kind=BF16: pltpu.VMEM(shape, kind)
    out, grad_one, grad_two = pl.pallas_call(
        kernel,
        out_shape=(
            jax.ShapeDtypeStruct((BAND, C), BF16),
            jax.ShapeDtypeStruct((9 * DPW * RW // 128, 128), F32),
            jax.ShapeDtypeStruct((9 * DPW * RW // 128, 128), F32),
        ),
        in_specs=[pl.BlockSpec(memory_space=pltpu.VMEM)] * 6,
        out_specs=[pl.BlockSpec(memory_space=pltpu.VMEM)] * 3,
        scratch_shapes=[
            vmem((PIX, C)),
            vmem((PIX + 2 * W, C)),
            vmem((C, K3)),
            vmem((C, K3)),
            vmem((PIX + 2 * W, C)),
            vmem((PIX, 256), F32),
            vmem((PIX, Q), F32),
            vmem((PIX, 256), F32),
            vmem((PIX, 256)),
            vmem((PIX + 2 * W, Q)),
            vmem((PIX + 2 * W, Q)),
            vmem((C, PIX)),
            vmem((C, PIX)),
            vmem((4, 2, BAND, C)),
            vmem((2, BAND, C)),
            vmem((2, 2, BAND, C)),
            vmem((BAND, C)),
            vmem((BAND, C)),
            vmem((PIX // 2, 128)),
            vmem((PIX // 2, 128)),
            vmem((4, PIX // 2, 128)),
            vmem((6, 8, 2, DPW, Q)),
            vmem((6, 8, DPW, Q)),
            vmem((6, 8, DPW, Q)),
            vmem((6, 2, DPW, Q)),
            vmem((6, 2, 2, DPW, Q)),
            vmem((6, DPW, Q)),
            vmem((6, DPW, Q)),
            vmem((3 * RANK, C)),
            vmem((3 * RANK, 256)),
            vmem((8, C), F32),
            vmem((8, C), F32),
            vmem((2, DPW, 128), F32),
            pltpu.SemaphoreType.DMA((N_SEM,)),
            pltpu.SemaphoreType.DMA((N_SEM,)),
        ],
        compiler_params=pltpu.CompilerParams(
            collective_id=0, has_side_effects=True, vmem_limit_bytes=66 * 1000 * 1000
        ),
    )(
        images.reshape(BAND, C),
        cotangent.reshape(BAND, C),
        first_weight.reshape(9, DPW, RW),
        second_weight.reshape(9, DPW, RW),
        first_basis,
        mine,
    )
    return (
        out.reshape(1, 3, W, C),
        grad_one.reshape(1, 1, 9, DPW * RW),
        grad_two.reshape(1, 1, 9, DPW * RW),
    )


def solution(mesh):
    return jax.shard_map(
        body,
        mesh=mesh,
        in_specs=(
            P("dp", "rows", None, None),
            P("dp", "rows", None, None),
            P("dp", "rows", None, None),
            P("dp", "rows", None, None),
            P(),
            P(),
        ),
        out_specs=(
            P("dp", "rows", None, None),
            P("dp", "rows", None, None),
            P("dp", "rows", None, None),
        ),
        check_vma=False,
    )
```

```python
import math

import jax
import jax.numpy as jnp
from jax import lax
from jax.experimental import pallas as pl
from jax.experimental.pallas import tpu as pltpu
from jax.sharding import PartitionSpec as P

C = 1280
GSIZE = 40
W = 48
H = 24
PIX = W * H
BAND = 144
DPW = 80
RW = 160
Q = 512
K3 = 3 * Q
RANK = 64
EPS = 1e-05
F32 = jnp.float32
BF16 = jnp.bfloat16
MESH = pl.DeviceIdType.MESH
HIGH = lax.Precision.HIGHEST
N_SEM = 124
PART = 288
AT = 384


def dot(a, b):
    return jnp.dot(a, b, preferred_element_type=F32)


def dot_nt(a, b):
    return lax.dot_general(a, b, (((1,), (1,)), ((), ())), preferred_element_type=F32)


def group_matrix(rows, channel_of):
    channel = channel_of(lax.broadcasted_iota(jnp.int32, (rows, 128), 0))
    group = lax.broadcasted_iota(jnp.int32, (rows, 128), 1) * GSIZE
    return jnp.where((channel >= group) & (channel < group + GSIZE), 1.0, 0.0).astype(F32)


def group_mean(sums, groups):
    per_group = jnp.sum(jnp.dot(sums, groups, precision=HIGH, preferred_element_type=F32), axis=0, keepdims=True)
    spread = lax.dot_general(
        jnp.broadcast_to(per_group, (8, 128)), groups, (((1,), (1,)), ((), ())),
        precision=HIGH, preferred_element_type=F32,
    )
    return spread[0:1] * (1.0 / (PIX * GSIZE))


def fold8(values):
    total = values[0:8]
    for at in range(8, values.shape[0], 8):
        total = total + values[at : at + 8]
    return total


def split(values):
    high = values.astype(BF16)
    low = (values - high.astype(F32)).astype(BF16)
    return high, low


def kernel(
    img, cot, w1r, w2r, b1, b2, out, g1, g2,
    imgf, cotp, w1, w2, actp, x, s, du, hidc, hp, pp, act_t, cot_t,
    o, qa, qb, qd, qv, hb, hx, hpair, gr, gc, gt, ga, gb, gd, gu, bs1, bs2, means, squares, flat,
    ssem, rsem,
):
    dp = lax.axis_index("dp")
    rows = lax.axis_index("rows")
    core = lax.rem(dp, 2)
    xh = lax.rem(dp // 2, 2)
    y = dp // 4
    xl = lax.rem(rows, 2)
    z = rows // 2
    zp, zm, z2 = lax.rem(z + 1, 4), lax.rem(z + 3, 4), lax.rem(z + 2, 4)
    yp, ym, y2 = lax.rem(y + 1, 4), lax.rem(y + 3, 4), lax.rem(y + 2, 4)
    ZP, ZM = (dp, zp * 2 + xl), (dp, zm * 2 + xl)
    XN = (dp, z * 2 + 1 - xl)
    YP, YM = (yp * 4 + xh * 2 + core, rows), (ym * 4 + xh * 2 + core, rows)
    XH = (y * 4 + (1 - xh) * 2 + core, rows)
    CN = (y * 4 + xh * 2 + 1 - core, rows)
    pending = []

    def send(src, dst, device):
        at = len(pending)
        copy = pltpu.make_async_remote_copy(
            src_ref=src, dst_ref=dst, send_sem=ssem.at[at], recv_sem=rsem.at[at],
            device_id=device, device_id_type=MESH,
        )
        copy.start()
        pending.append(copy)
        return copy

    def pass_on(piece, device):
        return send(piece, piece, device)

    def gather_rows(src, full, base):
        one, two = (0, 80), (80, 64)

        def at(zz, xx, part):
            return full.at[pl.ds(pl.multiple_of(base + (zz * 2 + xx) * BAND + part[0], 16), part[1])]

        def own(part, device):
            return send(src.at[pl.ds(part[0], part[1])], at(z, xl, part), device)

        cx = own(one, XN), own(two, XN)
        yield
        cp1, cm2, cp2, cm1 = own(one, ZP), own(two, ZM), own(two, ZP), own(one, ZM)
        yield
        cp1.wait_recv()
        fp = pass_on(at(zm, xl, one), ZP)
        cm2.wait_recv()
        fm = pass_on(at(zp, xl, two), ZM)
        yield
        cx[0].wait_recv()
        ep1, em1 = pass_on(at(z, 1 - xl, one), ZP), pass_on(at(z, 1 - xl, one), ZM)
        yield
        cx[1].wait_recv()
        ep2, em2 = pass_on(at(z, 1 - xl, two), ZP), pass_on(at(z, 1 - xl, two), ZM)
        yield
        cp2.wait_recv()
        cm1.wait_recv()
        yield
        ep1.wait_recv()
        hp_ = pass_on(at(zm, 1 - xl, one), ZP)
        em2.wait_recv()
        hm_ = pass_on(at(zp, 1 - xl, two), ZM)
        yield
        for copy in (fp, fm, ep2, em1):
            copy.wait_recv()
        yield
        hp_.wait_recv()
        hm_.wait_recv()
        yield

    def gather_rows_late(src, full, base):
        one, two, low, high = (0, 80), (80, 64), (0, 48), (48, 32)

        def at(zz, xx, part):
            return full.at[pl.ds(pl.multiple_of(base + (zz * 2 + xx) * BAND + part[0], 16), part[1])]

        def own(part, device):
            return send(src.at[pl.ds(part[0], part[1])], at(z, xl, part), device)

        cx = own(one, XN), own(two, XN)
        yield
        cp1, cm2, cp2, cm1 = own(one, ZP), own(two, ZM), own(two, ZP), own(one, ZM)
        yield
        cp1.wait_recv()
        fp = pass_on(at(zm, xl, one), ZP)
        cm2.wait_recv()
        fm = pass_on(at(zp, xl, two), ZM)
        gp = pass_on(at(zp, xl, two), XN)
        yield
        cx[0].wait_recv()
        ep, em = pass_on(at(z, 1 - xl, one), ZP), pass_on(at(z, 1 - xl, one), ZM)
        yield
        cp2.wait_recv()
        gm = pass_on(at(zm, xl, two), XN)
        yield
        cx[1].wait_recv()
        cm1.wait_recv()
        yield
        ep.wait_recv()
        hp_ = pass_on(at(zm, 1 - xl, low), ZP)
        em.wait_recv()
        hm_ = pass_on(at(zp, 1 - xl, high), ZM)
        fm.wait_recv()
        gf = pass_on(at(z2, xl, two), XN)
        yield
        for copy in (fp, gp, gm):
            copy.wait_recv()
        yield
        for copy in (hp_, hm_, gf):
            copy.wait_recv()
        yield

    def gather_weight(full):
        one, two, both = (0, 48), (48, 32), (0, DPW)

        def at(yy, hh, part=both):
            return full.at[pl.ds(pl.multiple_of(((yy * 2 + hh) * 2 + core) * DPW + part[0], 16), part[1])]

        last = []

        def to_core(yy, hh):
            last.append(pass_on(at(yy, hh), CN))

        ax = pass_on(at(y, xh, one), XH), pass_on(at(y, xh, two), XH)
        yield
        ap1, am2 = pass_on(at(y, xh, one), YP), pass_on(at(y, xh, two), YM)
        ap2, am1 = pass_on(at(y, xh, two), YP), pass_on(at(y, xh, one), YM)
        to_core(y, xh)
        yield
        ap1.wait_recv()
        fp = pass_on(at(ym, xh, one), YP)
        am2.wait_recv()
        fm = pass_on(at(yp, xh, two), YM)
        yield
        ax[0].wait_recv()
        bp1, bm1 = pass_on(at(y, 1 - xh, one), YP), pass_on(at(y, 1 - xh, one), YM)
        ax[1].wait_recv()
        bp2, bm2 = pass_on(at(y, 1 - xh, two), YP), pass_on(at(y, 1 - xh, two), YM)
        to_core(y, 1 - xh)
        yield
        ap2.wait_recv()
        to_core(ym, xh)
        am1.wait_recv()
        to_core(yp, xh)
        yield
        bp1.wait_recv()
        hp_ = pass_on(at(ym, 1 - xh, one), YP)
        bm2.wait_recv()
        hm_ = pass_on(at(yp, 1 - xh, two), YM)
        yield
        bp2.wait_recv()
        to_core(ym, 1 - xh)
        bm1.wait_recv()
        to_core(yp, 1 - xh)
        fp.wait_recv()
        fm.wait_recv()
        to_core(y2, xh)
        yield
        hp_.wait_recv()
        hm_.wait_recv()
        to_core(y2, 1 - xh)
        yield
        for copy in last:
            copy.wait_recv()
        yield

    scale = 1.0 / math.sqrt(16 * PIX)
    lane20 = lax.broadcasted_iota(jnp.int32, (20, 128), 1)

    def scatter_grad(n, grad_out, p):
        c = send(gr.at[n, :, 1 - core], gc.at[n], CN)
        yield
        c.wait_recv()
        for block in range(8):
            gt[n, block] = (gr[n, block, core].astype(F32) + gc[n, block].astype(F32)).astype(BF16)
        ap = send(gt.at[n, y2 * 2], ga.at[n, 0], YP)
        am = send(gt.at[n, y2 * 2 + 1], ga.at[n, 1], YM)
        yield
        ap.wait_recv()
        gt[n, yp * 2] = (gt[n, yp * 2].astype(F32) + ga[n, 0].astype(F32)).astype(BF16)
        bp = send(gt.at[n, pl.ds(yp * 2, 2)], gb.at[n, 0], YP)
        am.wait_recv()
        gt[n, ym * 2 + 1] = (gt[n, ym * 2 + 1].astype(F32) + ga[n, 1].astype(F32)).astype(BF16)
        bm = send(gt.at[n, pl.ds(ym * 2, 2)], gb.at[n, 1], YM)
        yield
        bp.wait_recv()
        bm.wait_recv()

        def mine(h):
            return gt[n, y * 2 + h].astype(F32) + gb[n, 0, h].astype(F32) + gb[n, 1, h].astype(F32)

        gu[n] = mine(1 - xh).astype(BF16)
        d = send(gu.at[n], gd.at[n], XH)
        yield
        d.wait_recv()
        total = (mine(xh) + gd[n].astype(F32)) * scale
        rest = total[:, 384:512]
        for q in range(3):
            turned = rest if q == 0 else pltpu.roll(rest, 128 - 32 * q, 1)
            flat[0] = total[:, q * 128 : q * 128 + 128]
            flat[1] = turned
            main = [flat[0, pl.ds(i, 20, stride=4)] for i in range(4)]
            tail = [flat[1, pl.ds(i, 20, stride=4)] for i in range(4)]
            pieces = [main[0]]
            for i in range(1, 4):
                shifted = pltpu.roll(main[i], 32 * i, 1)
                low = pltpu.roll(tail[i - 1], 32 * (i - 1), 1)
                low = jnp.where(lane20 < 32 * (i - 1), carried, low) if i > 1 else low
                pieces.append(jnp.where(lane20 < 32 * i, low, shifted))
                carried = shifted
            pieces.append(jnp.where(lane20 < 96, carried, pltpu.roll(tail[3], 96, 1)))
            for j in range(5):
                grad_out[pl.ds((p * 3 + q) * 100 + j, 20, stride=5)] = pieces[j]
        yield

    def step(*work):
        for one in work:
            next(one)

    barrier = pltpu.get_barrier_semaphore()
    for device in (ZP, ZM, XN, YP, YM, XH, CN):
        pl.semaphore_signal(barrier, inc=1, device_id=device, device_id_type=MESH)

    for raw, full in ((w1r, w1), (w2r, w2)):
        mine_at = pl.ds(pl.multiple_of(dp * DPW, 16), DPW)
        for p in range(3):
            rest = jnp.zeros((DPW, 128), F32)
            lane = lax.broadcasted_iota(jnp.int32, (DPW, 128), 1)
            for q in range(3):
                full[mine_at, p * Q + q * 128 : p * Q + q * 128 + 128] = raw[p * 3 + q, :, 0:128]
                tail = jnp.concatenate(
                    [raw[p * 3 + q, :, 128:160].astype(F32), jnp.zeros((DPW, 96), F32)], axis=1
                )
                rest = rest + (tail if q == 0 else pltpu.roll(tail, 32 * q, 1))
            full[mine_at, p * Q + 384 : p * Q + 512] = rest.astype(BF16)

    pl.semaphore_wait(barrier, 7)

    get_img = gather_rows(img, imgf, 0)
    get_w1 = gather_weight(w1)
    get_cot = gather_rows_late(cot, cotp, W)
    get_w2 = gather_weight(w2)
    step(get_w1, get_img, get_img, get_w1, get_w2, get_cot)

    imgf[pl.ds(pl.multiple_of(rows * BAND, 16), BAND)] = img[...]
    cotp[pl.ds(pl.multiple_of(W + rows * BAND, 16), BAND)] = cot[...]
    for buffer in (actp, cotp, hp, pp):
        buffer[0:W] = jnp.zeros((W, buffer.shape[1]), BF16)
        buffer[W + PIX : 2 * W + PIX] = jnp.zeros((W, buffer.shape[1]), BF16)
    for basis, held in ((b1, bs1), (b2, bs2)):
        high, low = split(basis[...])
        held[0:RANK] = high
        held[RANK : 2 * RANK] = low
        held[2 * RANK : 3 * RANK] = high

    def band_stats(slot, zz, xx):
        base = (zz * 2 + xx) * BAND

        def rows_of(i):
            return imgf[pl.ds(pl.multiple_of(base + i * 16, 16), 16)].astype(F32)

        total = lax.fori_loop(0, BAND // 16, lambda i, acc: acc + fold8(rows_of(i)), jnp.zeros((8, C), F32))
        mean = jnp.sum(total, axis=0, keepdims=True) * (1.0 / BAND)
        means[slot : slot + 1] = mean
        squares[...] = lax.fori_loop(
            0, BAND // 16, lambda i, acc: acc + fold8(jnp.square(rows_of(i) - mean)), squares[...]
        )

    squares[...] = jnp.zeros((8, C), F32)
    band_stats(0, z, xl)
    step(get_w1, get_img, get_w1, get_img, get_img)
    band_stats(1, z, 1 - xl)
    step(get_w1, get_w1, get_img)
    step(get_w2)
    band_stats(2, zm, xl)
    band_stats(3, zp, xl)
    step(get_img, get_cot)
    step(get_w1, get_w1)
    step(get_img)
    band_stats(4, z2, xl)
    band_stats(5, zm, 1 - xl)
    band_stats(6, zp, 1 - xl)
    step(get_w2, get_w2)
    step(get_img)
    band_stats(7, z2, 1 - xl)

    groups = group_matrix(C, lambda row: row)
    center = group_mean(means[...] * BAND, groups)
    total = squares[...] + BAND * jnp.square(means[...] - center)
    factor = lax.rsqrt(group_mean(total, groups) + EPS)

    def img_rows(i):
        return imgf[pl.ds(pl.multiple_of(i * 32, 16), 32)].astype(F32)

    def activate_rows(i, carry):
        u = (img_rows(i) - center) * factor
        actp[pl.ds(pl.multiple_of(W + i * 32, 16), 32)] = (u / (1.0 + jnp.exp(-u))).astype(BF16)
        return carry

    lax.fori_loop(0, PIX // 32, activate_rows, 0)
    step(get_cot, get_cot, get_w2, get_w2)
    step(get_w1)

    MT = 576

    def conv_tiles(source, weight, flip, begin=0, end=PIX // MT):
        def tile(i, carry):
            sums = None
            for p in range(3):
                first = (2 - p if flip else p) * W
                part = dot(
                    source[pl.ds(pl.multiple_of(first + i * MT, 16), MT)],
                    weight[:, p * Q : p * Q + Q],
                )
                sums = part if sums is None else sums + part
            s[pl.ds(pl.multiple_of(i * MT, 16), MT)] = sums
            return carry

        lax.fori_loop(begin, end, tile, 0)

    conv_tiles(actp, w1, False)
    step(get_w2, get_cot, get_cot, get_w2)

    col = lax.broadcasted_iota(jnp.int32, (PART // W, W, 128), 1).reshape(PART, 128)
    lane = lax.broadcasted_iota(jnp.int32, (PART, 128), 1)

    def row_at(h, base=0):
        return pl.ds(pl.multiple_of(base + h * PART, 16), PART)

    def from_left(v):
        return jnp.where(col >= 1, pltpu.roll(v, 1, 0), 0.0)

    def from_right(v):
        return jnp.where(col <= W - 2, pltpu.roll(v, PART - 1, 0), 0.0)

    def col_sum(h, first, last):
        part = s[row_at(h)]
        main = first(part[:, 0:128]) + part[:, 128:256] + last(part[:, 256:384])
        rest = part[:, 384:512]
        rest = first(rest) + pltpu.roll(rest, 96, 1) + pltpu.roll(last(rest), 64, 1)
        return main, jnp.where(lane < 32, rest, 0.0)

    def spread_cols(buffer, h, main, rest, first, last):
        at = row_at(h, W)
        buffer[at, 0:128] = first(main).astype(BF16)
        buffer[at, 128:256] = main.astype(BF16)
        buffer[at, 256:384] = last(main).astype(BF16)
        packed = first(rest) + pltpu.roll(rest, 32, 1) + pltpu.roll(last(rest), 64, 1)
        buffer[at, 384:512] = packed.astype(BF16)

    def sum_x(h, acc):
        main, rest = col_sum(h, from_left, from_right)
        x[row_at(h), 0:128] = main
        x[row_at(h), 128:256] = rest
        return acc + fold8(jnp.concatenate([main, rest], axis=1))

    zero_acc = jnp.zeros((8, 256), F32)
    groups_x = group_matrix(256, lambda row: row)
    real = lax.broadcasted_iota(jnp.int32, (1, 256), 1) < RW
    center_x = group_mean(lax.fori_loop(0, PIX // PART, sum_x, zero_acc), groups_x)

    def dev_x(h, acc):
        d = jnp.where(real, x[row_at(h)] - center_x, 0.0)
        return acc + fold8(d * d)

    factor_x = lax.rsqrt(group_mean(lax.fori_loop(0, PIX // PART, dev_x, zero_acc), groups_x) + EPS)

    def hidden_rows(h, carry):
        u = jnp.where(real, (x[row_at(h)] - center_x) * factor_x, 0.0)
        x[row_at(h)] = u
        a = u / (1.0 + jnp.exp(-u))
        hidc[row_at(h)] = a.astype(BF16)
        spread_cols(hp, h, a[:, 0:128], a[:, 128:256], from_left, from_right)
        return carry

    lax.fori_loop(0, PIX // PART, hidden_rows, 0)

    HALF = PIX // 2
    coef = dot_nt(hidc[...], bs2[0 : 2 * RANK])
    coef = coef[:, 0:RANK] + coef[:, RANK : 2 * RANK]
    hb[...] = jnp.concatenate([coef[0:HALF], coef[HALF:PIX]], axis=1).astype(BF16)
    hc0 = send(hb, hx, XN)

    def project_act(i, carry):
        a = actp[pl.ds(pl.multiple_of(W + i * AT, 16), AT)]
        c = dot_nt(a, bs1[0 : 2 * RANK])
        high, low = split(c[:, 0:RANK] + c[:, RANK : 2 * RANK])
        back = dot(jnp.concatenate([high, high, low], axis=1), bs1[...])
        left = (a.astype(F32) - back).astype(BF16)
        act_t[:, pl.ds(pl.multiple_of(i * AT, 128), AT)] = left.T
        return carry

    project_act(0, 0)
    step(get_cot)
    lax.fori_loop(1, PIX // AT, project_act, 0)

    GT = 1280

    def grad_tiles(n, left_t, buffer, first):
        def tile(i, carry):
            part = dot(left_t[pl.ds(pl.multiple_of(i * GT, 16), GT)], buffer[first : first + PIX])
            per = GT // (2 * DPW)
            gr[n, pl.ds(i * per, per)] = part.astype(BF16).reshape(per, 2, DPW, Q)
            return carry

        lax.fori_loop(0, C // GT, tile, 0)

    chunks = [scatter_grad(p, g1, p) for p in range(3)] + [scatter_grad(3 + p, g2, p) for p in range(3)]

    def move(*which):
        for one in which:
            next(chunks[one])

    def conv_second(zz):
        sums = None
        for p in range(3):
            part = dot_nt(hp[pl.ds(pl.multiple_of(p * W + zz * 288, 16), 288)], w2[:, p * Q : p * Q + Q])
            sums = part if sums is None else sums + part
        o[zz] = sums.astype(BF16).reshape(2, BAND, C)

    def add_into(target, extra):
        return (target.astype(F32) + extra.astype(F32)).astype(BF16)

    step(get_w2)
    step(get_cot, get_cot)

    conv_tiles(cotp, w2, True)
    hc0.wait_recv()
    hpair[z] = (hb[...].astype(F32) + hx[...].astype(F32)).astype(BF16)
    hcp = send(hpair.at[z], hpair.at[z], ZP)
    hcm = send(hpair.at[z], hpair.at[z], ZM)

    def grad_rows(h, carry):
        acc, acc_u = carry
        main, rest = col_sum(h, from_right, from_left)
        hg = jnp.concatenate([main, rest], axis=1)
        u = x[row_at(h)]
        sig = 1.0 / (1.0 + jnp.exp(-u))
        d = hg * (sig * (1.0 + u * (1.0 - sig)))
        du[row_at(h)] = d
        return acc + fold8(d), acc_u + fold8(d * u)

    acc, acc_u = lax.fori_loop(0, PIX // PART, grad_rows, (zero_acc, zero_acc))
    mean_d, mean_du = group_mean(acc, groups_x), group_mean(acc_u, groups_x)

    def pre_rows(h, carry):
        pre = factor_x * (du[row_at(h)] - mean_d - x[row_at(h)] * mean_du)
        pre = jnp.where(real, pre, 0.0)
        spread_cols(pp, h, pre[:, 0:128], pre[:, 128:256], from_right, from_left)
        return carry

    lax.fori_loop(0, PIX // PART, pre_rows, 0)


    grad_tiles(0, act_t, pp, 2 * W)
    move(0)
    conv_second(z2)
    hcp.wait_recv()
    hfp = send(hpair.at[zm, pl.ds(0, 288)], hpair.at[zm, pl.ds(0, 288)], ZP)
    hcm.wait_recv()
    hfm = send(hpair.at[zp, pl.ds(288, 288)], hpair.at[zp, pl.ds(288, 288)], ZM)
    oap, oam = send(o.at[z2, 0], qa.at[0], ZP), send(o.at[z2, 1], qa.at[1], ZM)
    move(0)
    grad_tiles(1, act_t, pp, W)
    move(1)
    conv_second(zp)
    move(1, 0)
    grad_tiles(2, act_t, pp, 0)
    move(2)
    conv_second(zm)
    move(2)
    oap.wait_recv()
    o[zp, 0] = add_into(o[zp, 0], qa[0])
    obp = send(o.at[zp], qb.at[0], ZP)
    oam.wait_recv()
    o[zm, 1] = add_into(o[zm, 1], qa[1])
    obm = send(o.at[zm], qb.at[1], ZM)
    move(1)

    hfp.wait_recv()
    hfm.wait_recv()

    def project_hidden(h, carry):
        part = hpair[0, row_at(h)].astype(F32)
        for zz in range(1, 4):
            part = part + hpair[zz, row_at(h)].astype(F32)
        for side in range(2):
            high, low = split(part[:, side * RANK : side * RANK + RANK])
            back = dot(jnp.concatenate([high, high, low], axis=1), bs2[...])
            hh = h + side * (HALF // PART)
            left = hidc[row_at(hh)].astype(F32) - back
            spread_cols(pp, hh, left[:, 0:128], left[:, 128:256], from_left, from_right)
        return carry

    lax.fori_loop(0, HALF // PART, project_hidden, 0)

    def turn_cot(i, carry):
        cot_t[:, pl.ds(pl.multiple_of(i * 128, 128), 128)] = cotp[
            pl.ds(pl.multiple_of(W + i * 128, 16), 128)
        ].T
        return carry

    lax.fori_loop(0, PIX // 128, turn_cot, 0)

    move(0)
    grad_tiles(3, cot_t, pp, 0)
    move(3, 2)
    conv_second(z)
    move(3, 1)
    grad_tiles(4, cot_t, pp, W)
    move(4, 0, 4, 3, 2)
    grad_tiles(5, cot_t, pp, 2 * W)
    move(5, 1, 5, 4)

    def band(xx):
        return o[z, xx].astype(F32) + qb[0, xx].astype(F32) + qb[1, xx].astype(F32)

    obp.wait_recv()
    obm.wait_recv()
    qv[...] = band(1 - xl).astype(BF16)
    odx = send(qv, qd, XN)
    move(2, 3, 5, 4, 5)
    odx.wait_recv()
    out[...] = (img[...].astype(F32) + (band(xl) + qd[...].astype(F32))).astype(BF16)
    move(3, 4, 5)
    for copy in pending:
        copy.wait_send()


def body(images, cotangent, first_weight, second_weight, first_basis, second_basis):
    mine = lax.dynamic_slice_in_dim(second_basis, lax.axis_index("rows") * RW, RW, 1)
    mine = jnp.pad(mine, ((0, 0), (0, 256 - RW)))
    vmem = lambda shape, kind=BF16: pltpu.VMEM(shape, kind)
    out, grad_one, grad_two = pl.pallas_call(
        kernel,
        out_shape=(
            jax.ShapeDtypeStruct((BAND, C), BF16),
            jax.ShapeDtypeStruct((9 * DPW * RW // 128, 128), F32),
            jax.ShapeDtypeStruct((9 * DPW * RW // 128, 128), F32),
        ),
        in_specs=[pl.BlockSpec(memory_space=pltpu.VMEM)] * 6,
        out_specs=[pl.BlockSpec(memory_space=pltpu.VMEM)] * 3,
        scratch_shapes=[
            vmem((PIX, C)),
            vmem((PIX + 2 * W, C)),
            vmem((C, K3)),
            vmem((C, K3)),
            vmem((PIX + 2 * W, C)),
            vmem((PIX, 256), F32),
            vmem((PIX, Q), F32),
            vmem((PIX, 256), F32),
            vmem((PIX, 256)),
            vmem((PIX + 2 * W, Q)),
            vmem((PIX + 2 * W, Q)),
            vmem((C, PIX)),
            vmem((C, PIX)),
            vmem((4, 2, BAND, C)),
            vmem((2, BAND, C)),
            vmem((2, 2, BAND, C)),
            vmem((BAND, C)),
            vmem((BAND, C)),
            vmem((PIX // 2, 128)),
            vmem((PIX // 2, 128)),
            vmem((4, PIX // 2, 128)),
            vmem((6, 8, 2, DPW, Q)),
            vmem((6, 8, DPW, Q)),
            vmem((6, 8, DPW, Q)),
            vmem((6, 2, DPW, Q)),
            vmem((6, 2, 2, DPW, Q)),
            vmem((6, DPW, Q)),
            vmem((6, DPW, Q)),
            vmem((3 * RANK, C)),
            vmem((3 * RANK, 256)),
            vmem((8, C), F32),
            vmem((8, C), F32),
            vmem((2, DPW, 128), F32),
            pltpu.SemaphoreType.DMA((N_SEM,)),
            pltpu.SemaphoreType.DMA((N_SEM,)),
        ],
        compiler_params=pltpu.CompilerParams(
            collective_id=0, has_side_effects=True, vmem_limit_bytes=66 * 1000 * 1000
        ),
    )(
        images.reshape(BAND, C),
        cotangent.reshape(BAND, C),
        first_weight.reshape(9, DPW, RW),
        second_weight.reshape(9, DPW, RW),
        first_basis,
        mine,
    )
    return (
        out.reshape(1, 3, W, C),
        grad_one.reshape(1, 1, 9, DPW * RW),
        grad_two.reshape(1, 1, 9, DPW * RW),
    )


def solution(mesh):
    return jax.shard_map(
        body,
        mesh=mesh,
        in_specs=(
            P("dp", "rows", None, None),
            P("dp", "rows", None, None),
            P("dp", "rows", None, None),
            P("dp", "rows", None, None),
            P(),
            P(),
        ),
        out_specs=(
            P("dp", "rows", None, None),
            P("dp", "rows", None, None),
            P("dp", "rows", None, None),
        ),
        check_vma=False,
    )
```
